32 devices in a mesh: runs: 2 (over y), mem: 4 (over x, core), lat: 4 (over z).
Axes of the slice: x: 2, y: 2, z: 4, core: 2. Of those that a mesh axis runs over, the one named last changes fastest.
Arguments:
- states: bfloat16 [8, 12, 160, 768], P(('runs', 'mem'), 'lat'), parts along dimension 0, may hold values from -6 to 6
- land_mask: int32 [12, 768], P('lat'), may hold values 0 or 1
- cutoff: int32 [12], replicated, may hold values from 48 to 383
- kernel: float32 [7, 7, 160], replicated, may hold values from -0.875 to 0.875
- norm_gain: float32 [160], replicated, may hold values from 0.5 to 2
- norm_bias: float32 [160], replicated, may hold values from -3 to 3
- weight_in: bfloat16 [160, 640], replicated, may hold values from -0.5 to 0.5
- bias_in: float32 [640], replicated, may hold values from -4 to 4
- weight_out: bfloat16 [640, 160], replicated, may hold values from -0.25 to 0.25
Outputs:
- advanced: bfloat16 [8, 12, 160, 768], P(('runs', 'mem'), 'lat'), parts along dimension 0
The draws below stay inside these ranges and needn't reach their ends.
There are 2 independent parts, one for each index of `runs`. The reference program is written for one: setup_inputs(seed, part) draws one part's arguments, and reference() takes and returns one part's arrays. A program takes and returns all parts, laid end to end along the dimension named above; an argument that names none is the same for every part. Nothing has to cross between parts.
All inputs are finite; a program needn't handle non-finite values. No bound on the sum of `land_mask` on one device may be relied on, other than what follows from the above.
Results may differ from the reference program's by a relative error of at most 0.012.
Values may be sent and summed in bfloat16 or wider, within the bound.
No kernel may reach another device: no remote copies, remote signals or barrier semaphores. Data moves between devices by JAX's collectives and lax.ppermute only.
A program may use at most 64 MiB of HBM per device.

```python
import math
import jax
import jax.numpy as jnp
from jax import lax

C = 160
HID = 640
W = 768
STEPS = 2
POLAR = 6
LAT = 12
MEMBERS = 4


def place_ends(result, own_key, smallest, largest):
    longest = result.shape.index(max(result.shape))
    spots = []
    for shift in (0, 1):
        where = [jax.random.randint(jax.random.fold_in(own_key, axis), (), 0, length) for axis, length in enumerate(result.shape)]
        where[longest] = (where[longest] + shift) % result.shape[longest]
        spots.append(tuple(where))
    return result.at[spots[0]].set(smallest).at[spots[1]].set(largest)


def block_levels(rng, dims, shards, low, high):
    factor_of = 1.0
    for axis_at, blocks in shards:
        steps = jax.random.uniform(jax.random.fold_in(jax.random.fold_in(rng, 6), axis_at), (blocks,), jnp.float32, low / len(shards), high / len(shards))
        factor_of = factor_of * jnp.repeat(jnp.exp(steps), dims[axis_at] // blocks).reshape((-1,) + (1,) * (len(dims) - 1 - axis_at))
    return factor_of


def bell_draw(rng, dims, spread, limit, shards=(), kind=jnp.bfloat16):
    entries = spread * jax.random.normal(rng, dims, jnp.float32)
    if shards:
        entries = entries * block_levels(rng, dims, shards, -0.22, 0.18)
    return jnp.clip(entries, -limit, limit).astype(kind)


def setup_inputs(seed: int = 0, part: int = 0) -> dict:
    arg_keys = jax.random.split(jax.random.key(seed), 10)
    part_keys = jax.random.split(jax.random.fold_in(arg_keys[9], part), 10)
    return {
        "states": bell_draw(part_keys[0], (MEMBERS, LAT, C, W), 1.0, 6.0, ((0, 4), (1, 4))),
        "land_mask": place_ends((jax.random.randint(arg_keys[1], (LAT, W), 0, 10) < 7).astype(jnp.int32), jax.random.fold_in(arg_keys[1], 1), 0, 1),
        "cutoff": place_ends(jax.random.randint(arg_keys[2], (2 * POLAR,), W // 16, W // 2), jax.random.fold_in(arg_keys[2], 1), W // 16, (W // 2) - 1).astype(jnp.int32),
        "kernel": bell_draw(arg_keys[3], (7, 7, C), 49 ** -0.5, 0.875, (), jnp.float32),
        "norm_gain": jnp.clip(jnp.exp(jax.random.uniform(arg_keys[4], (C,), jnp.float32, math.log(0.5), math.log(2.0))), 0.5, 2.0),
        "norm_bias": bell_draw(arg_keys[5], (C,), 0.5, 3.0, (), jnp.float32),
        "weight_in": bell_draw(arg_keys[6], (C, HID), C ** -0.5, 0.5),
        "bias_in": bell_draw(arg_keys[7], (HID,), 1.0, 4.0, (), jnp.float32),
        "weight_out": bell_draw(arg_keys[8], (HID, C), HID ** -0.5, 0.25),
    }


gelu_scale = 0.7978845608028654
gelu_cubic = 0.044715
epsilon = 1e-05

def fourier(width):
    index = jnp.arange(width, dtype=jnp.int32)
    wavenumber = jnp.where(index <= width // 2, index, index - width // 2)
    phase = index[:, None] * wavenumber[None, :] % width
    angle = phase.astype(jnp.float32) * (2.0 * math.pi / width)
    factor = jnp.where((index == 0) | (index == width // 2), 1.0 / math.sqrt(width), math.sqrt(2.0 / width)).astype(jnp.float32)
    table = jnp.where(index[None, :] <= width // 2, jnp.cos(angle), jnp.sin(angle)) * factor[None, :]
    return (table.astype(jnp.bfloat16), wavenumber)

def gelu_pair(hidden):
    inner = jnp.tanh(gelu_scale * (hidden + gelu_cubic * hidden * hidden * hidden))
    value = 0.5 * hidden * (1.0 + inner)
    slope = 0.5 * (1.0 + inner) + 0.5 * hidden * (1.0 - inner * inner) * gelu_scale * (1.0 + 3.0 * gelu_cubic * hidden * hidden)
    return (value, slope)

def depthwise(field, kernel):
    rows = field.shape[0]
    padded = jnp.pad(field, ((3, 3), (0, 0), (0, 0)))
    total = jnp.zeros(field.shape, jnp.float32)
    for left in range(7):
        for right in range(7):
            total = total + kernel[left, right][:, None] * jnp.roll(padded[left:left + rows], 3 - right, axis=2)
    return total

def polar_filter(block, limits, table, wavenumber):
    keep = (wavenumber[None, :] <= limits[:, None]).astype(jnp.float32)
    spectrum = jnp.einsum('rcw,wk->rck', block.astype(jnp.float32), table.astype(jnp.float32)) * keep[:, None, :]
    spectrum = spectrum.astype(jnp.bfloat16)
    return jnp.einsum('rck,wk->rcw', spectrum.astype(jnp.float32), table.astype(jnp.float32)).astype(jnp.bfloat16)

def finish(member, mix, weight_out, land, cutoff, table, wavenumber):
    rows = member.shape[0]
    update = jnp.einsum('hc,rhw->rcw', weight_out.astype(jnp.float32), mix.astype(jnp.float32))
    unfiltered = (land[:, None, :] * (member.astype(jnp.float32) + update)).astype(jnp.bfloat16)
    polar = jnp.concatenate([unfiltered[:POLAR], unfiltered[rows - POLAR:]], axis=0)
    back = polar_filter(polar, cutoff, table, wavenumber)
    return jnp.concatenate([back[:POLAR], unfiltered[POLAR:rows - POLAR], back[POLAR:]], axis=0)

def reference(states, land_mask, cutoff, kernel, norm_gain, norm_bias, weight_in, bias_in, weight_out):
    table, wavenumber = fourier(states.shape[3])
    land = land_mask.astype(jnp.float32)
    control = states[0]
    tangents = states[1:]
    gain = norm_gain[None, :, None]
    for step in range(STEPS):
        control_conv = depthwise(control.astype(jnp.float32), kernel)
        centered = control_conv - lax.optimization_barrier(jnp.mean(control_conv, axis=1, keepdims=True))
        scale = lax.rsqrt(lax.optimization_barrier(jnp.mean(centered * centered, axis=1, keepdims=True)) + epsilon)
        unit = centered * scale
        normed = (unit * gain + norm_bias[None, :, None]).astype(jnp.bfloat16)
        hidden = jnp.einsum('ch,rcw->rhw', weight_in.astype(jnp.float32), normed.astype(jnp.float32)) + bias_in[None, :, None]
        value, slope = gelu_pair(hidden)
        activation = value.astype(jnp.bfloat16)

        def propagate(tangent):
            tangent_conv = depthwise(tangent.astype(jnp.float32), kernel)
            average = lax.optimization_barrier(jnp.mean(tangent_conv, axis=1, keepdims=True))
            along = lax.optimization_barrier(jnp.mean(tangent_conv * unit, axis=1, keepdims=True))
            tangent_normed = (gain * scale * (tangent_conv - average - unit * along)).astype(jnp.bfloat16)
            tangent_hidden = jnp.einsum('ch,rcw->rhw', weight_in.astype(jnp.float32), tangent_normed.astype(jnp.float32))
            tangent_mix = (slope * tangent_hidden).astype(jnp.bfloat16)
            return finish(tangent, tangent_mix, weight_out, land, cutoff, table, wavenumber)
        tangents = lax.map(propagate, tangents)
        control = finish(control, activation, weight_out, land, cutoff, table, wavenumber)
    return jnp.concatenate([control[None], tangents], axis=0)
```

```python
import math

import jax
import jax.numpy as jnp
import numpy as np
from jax import lax
from jax.experimental import pallas as pl
from jax.experimental.pallas import tpu as pltpu
from jax.sharding import PartitionSpec as P

STEPS = 2
POLAR = 6
HALO = 3
TAPS = 7
GROUP = 16

gelu_scale = 0.7978845608028654
gelu_cubic = 0.044715
epsilon = 1e-05


def fourier(width):
    index = np.arange(width, dtype=np.int32)
    wavenumber = np.where(index <= width // 2, index, index - width // 2).astype(np.int32)
    phase = index[:, None] * wavenumber[None, :] % width
    angle = phase.astype(np.float64) * (2.0 * math.pi / width)
    factor = np.where((index == 0) | (index == width // 2), 1.0 / math.sqrt(width), math.sqrt(2.0 / width))
    table = np.where(index[None, :] <= width // 2, np.cos(angle), np.sin(angle)) * factor[None, :]
    return table.astype(np.float32).astype(jnp.bfloat16), wavenumber


def tap_matrix(kernel, rows):
    channels = kernel.shape[2]
    groups = channels // GROUP
    shifted = jnp.stack([jnp.pad(kernel, ((r, rows - 1 - r), (0, 0), (0, 0))) for r in range(rows)])
    shifted = shifted.transpose(3, 2, 0, 1).reshape(groups, GROUP, TAPS, rows, rows + 2 * HALO)
    shifted = shifted.transpose(0, 2, 3, 1, 4)
    high = shifted.astype(jnp.bfloat16)
    low = (shifted - high.astype(jnp.float32)).astype(jnp.bfloat16)
    eye = jnp.eye(GROUP, dtype=jnp.bfloat16)
    both = jnp.stack([high, low], axis=4)
    full = both[..., None] * eye[:, None, None, :]
    return full.reshape(groups, TAPS * rows * GROUP, 2 * (rows + 2 * HALO) * GROUP)


def convolve(up, own, down, taps, out):
    rows, channels, width = out.shape

    def group(b, _):
        at = pl.ds(pl.multiple_of(b * GROUP, GROUP), GROUP)
        field = jnp.concatenate([up[:, at, :], own[:, at, :], down[:, at, :]], axis=0)
        field = field.reshape((rows + 2 * HALO) * GROUP, width)
        field = jnp.concatenate([field, field], axis=0)
        parts = jnp.dot(taps[b], field, preferred_element_type=jnp.float32)
        size = rows * GROUP
        total = parts[HALO * size : (HALO + 1) * size]
        for j in range(TAPS):
            if j != HALO:
                total = total + pltpu.roll(parts[j * size : (j + 1) * size], (HALO - j) % width, 1)
        out[:, at, :] = total.reshape(rows, GROUP, width)
        return 0

    lax.fori_loop(0, channels // GROUP, group, 0)


def polar_filter(raw, keep, polar, table, out, select):
    rows, channels, width = out.shape
    spectrum = jnp.dot(raw[...], table[...], preferred_element_type=jnp.float32)
    parts = [
        (spectrum[r * channels : (r + 1) * channels] * keep[r : r + 1, :]).astype(jnp.bfloat16) for r in range(rows)
    ]
    back = lax.dot_general(
        jnp.concatenate(parts, axis=0), table[...], (((1,), (1,)), ((), ())), preferred_element_type=jnp.float32
    ).astype(jnp.bfloat16)
    for r in range(rows):
        row = back[r * channels : (r + 1) * channels]
        if select:
            row = jnp.where(polar[r] > 0, row, raw[r * channels : (r + 1) * channels, :])
        out[r] = row


LANES = 256
CHUNK = 16


def control_kernel(
    select, polar, up, own, down, taps, gain, bias, w_in, b_in, w_out, land, keep, table,
    out, unit_out, scale_out, slope_out, conv, normed, hidden, act, raw,
):
    rows, channels, width = out.shape
    hid = w_in.shape[0]
    convolve(up, own, down, taps, conv)
    for r in range(rows):
        for w in range(0, width, LANES):
            at = slice(w, w + LANES)
            value = conv[r, :, at]
            centered = value - jnp.mean(value, axis=0, keepdims=True)
            scale = lax.rsqrt(jnp.mean(centered * centered, axis=0, keepdims=True) + epsilon)
            unit = centered * scale
            unit_out[r, :, at] = unit
            scale_out[r, :, at] = scale
            normed[:, at] = (unit * gain[...] + bias[...]).astype(jnp.bfloat16)
        hidden[...] = jnp.dot(w_in[...], normed[...], preferred_element_type=jnp.float32)

        def pair(c, _):
            at = pl.ds(pl.multiple_of(c * CHUNK, CHUNK), CHUNK)
            h = hidden[at, :] + b_in[at, :]
            square = h * h
            t = jnp.tanh(h * (gelu_scale + (gelu_scale * gelu_cubic) * square))
            half = 0.5 + 0.5 * t
            act[at, :] = (h * half).astype(jnp.bfloat16)
            slope = half + (0.5 * h) * (1.0 - t * t) * (gelu_scale + (3.0 * gelu_scale * gelu_cubic) * square)
            slope_out[r, at, :] = slope
            return 0

        lax.fori_loop(0, hid // CHUNK, pair, 0)
        update = jnp.dot(w_out[...], act[...], preferred_element_type=jnp.float32)
        raw[r * channels : (r + 1) * channels, :] = (
            land[r : r + 1, :] * (own[r].astype(jnp.float32) + update)
        ).astype(jnp.bfloat16)
    polar_filter(raw, keep, polar, table, out, select)


def tangent_kernel(
    select, polar, up, own, down, taps, gain, w_in, w_out, land, keep, table, unit_in, scale_in, slope_in, advanced,
    out, conv, normed, hidden, act, raw,
):
    rows, channels, width = out.shape
    hid = w_in.shape[0]
    is_control = polar[rows] > 0

    @pl.when(is_control)
    def _():
        out[...] = advanced[...]

    @pl.when(jnp.logical_not(is_control))
    def _():
        convolve(up, own, down, taps, conv)
        for r in range(rows):
            for w in range(0, width, LANES):
                at = slice(w, w + LANES)
                value = conv[r, :, at]
                unit = unit_in[r, :, at]
                average = jnp.mean(value, axis=0, keepdims=True)
                along = jnp.mean(value * unit, axis=0, keepdims=True)
                normed[:, at] = (gain[...] * scale_in[r, :, at] * (value - average - unit * along)).astype(jnp.bfloat16)
            hidden[...] = jnp.dot(w_in[...], normed[...], preferred_element_type=jnp.float32)

            def mix(c, _):
                at = pl.ds(pl.multiple_of(c * CHUNK, CHUNK), CHUNK)
                act[at, :] = (slope_in[r, at, :] * hidden[at, :]).astype(jnp.bfloat16)
                return 0

            lax.fori_loop(0, hid // CHUNK, mix, 0)
            update = jnp.dot(w_out[...], act[...], preferred_element_type=jnp.float32)
            raw[r * channels : (r + 1) * channels, :] = (
                land[r : r + 1, :] * (own[r].astype(jnp.float32) + update)
            ).astype(jnp.bfloat16)
        polar_filter(raw, keep, polar, table, out, select)


def scratch(rows, channels, width, hid):
    return [
        pltpu.VMEM((rows, channels, width), jnp.float32),
        pltpu.VMEM((channels, width), jnp.bfloat16),
        pltpu.VMEM((hid, width), jnp.float32),
        pltpu.VMEM((hid, width), jnp.bfloat16),
        pltpu.VMEM((rows * channels, width), jnp.bfloat16),
    ]


SMEM = pl.BlockSpec(memory_space=pltpu.SMEM)
VMEM = pl.BlockSpec(memory_space=pltpu.VMEM)
LIMIT = 48 << 20


def per_device(
    states, land_mask, cutoff, kernel, norm_gain, norm_bias, weight_in, bias_in, weight_out
):
    member = states[0]
    rows, channels, width = member.shape
    hid = weight_in.shape[1]
    bands = lax.axis_size("lat")
    members = lax.axis_size("mem")
    total_rows = rows * bands
    me = lax.axis_index("mem")
    select = total_rows > 2 * POLAR

    table, wavenumber = fourier(width)
    row = lax.axis_index("lat") * rows + jnp.arange(rows)
    is_polar = (row < POLAR) | (row >= total_rows - POLAR)
    place = jnp.clip(jnp.where(row < POLAR, row, row - total_rows + 2 * POLAR), 0, 2 * POLAR - 1)
    keep = (jnp.asarray(wavenumber)[None, :] <= cutoff[place][:, None]).astype(jnp.float32)
    flags = jnp.concatenate([is_polar.astype(jnp.int32), (me == 0).astype(jnp.int32)[None]])
    land = land_mask.astype(jnp.float32)
    taps = tap_matrix(kernel, rows)
    w_in = weight_in.T
    w_out = weight_out.T
    gain = norm_gain[:, None]
    offset = norm_bias[:, None]
    shift_in = bias_in[:, None]
    table = jnp.asarray(table)

    forward = [(i, i + 1) for i in range(bands - 1)]
    backward = [(i + 1, i) for i in range(bands - 1)]

    def spread(block):
        count = 2
        while count < members:
            sent = lax.ppermute(block, "mem", [(i, i + count) for i in range(0, count, 2) if i + count < members])
            block = jnp.where((me >= count) & (me < 2 * count), sent, block)
            count *= 2
        sent = lax.ppermute(block, "mem", [(i, i + 1) for i in range(0, members - 1, 2)])
        return jnp.where(me % 2 == 1, sent, block)

    params = pltpu.CompilerParams(vmem_limit_bytes=LIMIT)
    field = jax.ShapeDtypeStruct((rows, channels, width), jnp.bfloat16)

    def control_step(up, own, down):
        return pl.pallas_call(
            lambda *refs: control_kernel(select, *refs),
            out_shape=(
                field,
                jax.ShapeDtypeStruct((rows, channels, width), jnp.float32),
                jax.ShapeDtypeStruct((rows, 1, width), jnp.float32),
                jax.ShapeDtypeStruct((rows, hid, width), jnp.float32),
            ),
            in_specs=[SMEM] + [VMEM] * 12,
            out_specs=(VMEM,) * 4,
            scratch_shapes=scratch(rows, channels, width, hid),
            compiler_params=params,
            name="control",
        )(flags, up, own, down, taps, gain, offset, w_in, shift_in, w_out, land, keep, table)

    def tangent_step(up, own, down, unit, scale, slope, advanced):
        return pl.pallas_call(
            lambda *refs: tangent_kernel(select, *refs),
            out_shape=field,
            in_specs=[SMEM] + [VMEM] * 14,
            out_specs=VMEM,
            scratch_shapes=scratch(rows, channels, width, hid),
            compiler_params=params,
            name="tangent",
        )(flags, up, own, down, taps, gain, w_in, w_out, land, keep, table, unit, scale, slope, advanced)

    control = spread(member)
    for step in range(STEPS):
        up = lax.ppermute(member, "lat", forward)
        down = lax.ppermute(member, "lat", backward)
        control_up = spread(up)
        control_down = spread(down)
        control, unit, scale, slope = control_step(control_up, control, control_down)
        member = tangent_step(up, member, down, unit, scale, slope, control)
    return member[None]


def solution(mesh):
    in_specs = (
        P(("runs", "mem"), "lat", None, None),
        P("lat", None),
        P(),
        P(),
        P(),
        P(),
        P(),
        P(),
        P(),
    )
    out_specs = P(("runs", "mem"), "lat", None, None)
    return jax.shard_map(
        per_device, mesh=mesh, in_specs=in_specs, out_specs=out_specs, check_vma=False
    )
```

```python
import math

import jax
import jax.numpy as jnp
import numpy as np
from jax import lax
from jax.experimental import pallas as pl
from jax.experimental.pallas import tpu as pltpu
from jax.sharding import PartitionSpec as P

STEPS = 2
POLAR = 6
HALO = 3
TAPS = 7
GROUP = 16
LANES = 128
CHUNK = 16
BIAS_ROWS = 16

gelu_scale = 0.7978845608028654
gelu_cubic = 0.044715
epsilon = 1e-05

f32 = jnp.float32
bf16 = jnp.bfloat16


def fourier(width):
    index = np.arange(width, dtype=np.int32)
    wavenumber = np.where(index <= width // 2, index, index - width // 2).astype(np.int32)
    phase = index[:, None] * wavenumber[None, :] % width
    angle = phase.astype(np.float64) * (2.0 * math.pi / width)
    factor = np.where((index == 0) | (index == width // 2), 1.0 / math.sqrt(width), math.sqrt(2.0 / width))
    table = np.where(index[None, :] <= width // 2, np.cos(angle), np.sin(angle)) * factor[None, :]
    return table.astype(np.float32).astype(bf16), wavenumber


def unroll(count, most):
    return max(u for u in range(1, most + 1) if count % u == 0)


def prepare_kernel(kernel, gain, offset, taps, gain_out, offset_out):
    rows, _, channels, depth = taps.shape
    lane = lax.broadcasted_iota(jnp.int32, (channels, depth), 1)
    here = lax.broadcasted_iota(jnp.int32, (channels, depth), 0)
    own = lane % GROUP == here % GROUP
    for j in range(TAPS):
        columns = [jnp.broadcast_to(kernel[j, :, i : i + 1], (channels, depth)) for i in range(TAPS)]
        for r in range(rows):
            total = jnp.zeros((channels, depth), f32)
            for i in range(TAPS):
                total = jnp.where(own & (lane // GROUP == r + i), columns[i], total)
            taps[r, j] = total.astype(bf16)
    gain_out[...] = jnp.broadcast_to(gain[...], gain_out.shape)
    offset_out[...] = jnp.broadcast_to(offset[...], offset_out.shape)


def convolve(up, own, down, taps, out):
    rows, channels, width = out.shape

    def group(b, _):
        at = pl.ds(pl.multiple_of(b * GROUP, GROUP), GROUP)
        field = jnp.concatenate([up[:, at, :], own[:, at, :], down[:, at, :]], axis=0)
        field = field.reshape((rows + 2 * HALO) * GROUP, width)
        parts = jnp.dot(taps[:, :, at, :].reshape(rows * TAPS * GROUP, field.shape[0]), field, preferred_element_type=f32)
        for r in range(rows):
            part = [parts[(r * TAPS + j) * GROUP : (r * TAPS + j + 1) * GROUP] for j in range(TAPS)]
            total = part[HALO]
            for j in range(TAPS):
                if j != HALO:
                    total = total + pltpu.roll(part[j], (HALO - j) % width, 1)
            out[r, at, :] = total
        return 0

    groups = channels // GROUP
    lax.fori_loop(0, groups, group, 0, unroll=unroll(groups, 5))


def add_bias_rows(normed, channels):
    width = normed.shape[1]
    row = lax.broadcasted_iota(jnp.int32, (BIAS_ROWS, width), 0)
    normed[channels:, :] = jnp.where(row < 3, 1.0, 0.0).astype(bf16)


def polar_filter(raw, keep, polar, table, out, select):
    rows, channels, width = out.shape
    spectrum = jnp.dot(raw[...], table[...], preferred_element_type=f32)
    parts = [(spectrum[r * channels : (r + 1) * channels] * keep[r : r + 1, :]).astype(bf16) for r in range(rows)]
    back = lax.dot_general(
        jnp.concatenate(parts, axis=0), table[...], (((1,), (1,)), ((), ())), preferred_element_type=f32
    ).astype(bf16)
    for r in range(rows):
        row = back[r * channels : (r + 1) * channels]
        if select:
            row = jnp.where(polar[r] > 0, row, raw[r * channels : (r + 1) * channels, :])
        out[r] = row


def control_kernel(
    select, advance_all, polar, up, own, down, taps, gain, bias, w_in, w_out, land, keep, table,
    out, unit_out, scale_out, slope_out, conv, normed, hidden, act, raw,
):
    rows, channels, width = out.shape
    hid = w_in.shape[0]
    add_bias_rows(normed, channels)
    convolve(up, own, down, taps, conv)
    for r in range(rows):
        for w in range(0, width, LANES):
            at = slice(w, w + LANES)
            value = conv[r, :, at]
            centered = value - jnp.mean(value, axis=0, keepdims=True)
            scale = lax.rsqrt(jnp.mean(centered * centered, axis=0, keepdims=True) + epsilon)
            unit = centered * scale
            unit_out[r, :, at] = unit
            scale_out[r, :, at] = scale
            normed[:channels, at] = (unit * gain[...] + bias[...]).astype(bf16)
        hidden[...] = jnp.dot(w_in[...], normed[...], preferred_element_type=f32)

        def pair(c, _):
            at = pl.ds(pl.multiple_of(c * CHUNK, CHUNK), CHUNK)
            h = hidden[at, :]
            square = h * h
            t = jnp.tanh(h * (gelu_scale + (gelu_scale * gelu_cubic) * square))
            half = 0.5 + 0.5 * t
            act[at, :] = (h * half).astype(bf16)
            lean = h * (2.0 * gelu_scale + (6.0 * gelu_scale * gelu_cubic) * square)
            slope_out[r, at, :] = half * (1.0 + (1.0 - half) * lean)
            return 0

        lax.fori_loop(0, hid // CHUNK, pair, 0, unroll=unroll(hid // CHUNK, 5))
        update = jnp.dot(w_out[...], act[...], preferred_element_type=f32)
        raw[r * channels : (r + 1) * channels, :] = (land[r : r + 1, :] * (own[r].astype(f32) + update)).astype(bf16)
    polar_filter(raw, keep, polar, table, out, select)


def tangent_kernel(
    select, polar, up, own, down, taps, gain, w_in, w_out, land, keep, table, unit_in, scale_in, slope_in, advanced,
    out, conv, normed, hidden, act, raw,
):
    rows, channels, width = out.shape
    hid = w_in.shape[0]
    is_control = polar[rows] > 0

    @pl.when(is_control)
    def _():
        out[...] = advanced[...]

    @pl.when(jnp.logical_not(is_control))
    def _():
        convolve(up, own, down, taps, conv)
        for r in range(rows):
            for w in range(0, width, LANES):
                at = slice(w, w + LANES)
                value = conv[r, :, at]
                unit = unit_in[r, :, at]
                average = jnp.mean(value, axis=0, keepdims=True)
                along = jnp.mean(value * unit, axis=0, keepdims=True)
                normed[:channels, at] = (gain[...] * scale_in[r, :, at] * (value - average - unit * along)).astype(bf16)
            hidden[...] = jnp.dot(w_in[:, :channels], normed[:channels, :], preferred_element_type=f32)

            def mix(c, _):
                at = pl.ds(pl.multiple_of(c * CHUNK, CHUNK), CHUNK)
                act[at, :] = (slope_in[r, at, :] * hidden[at, :]).astype(bf16)
                return 0

            lax.fori_loop(0, hid // CHUNK, mix, 0, unroll=unroll(hid // CHUNK, 5))
            update = jnp.dot(w_out[...], act[...], preferred_element_type=f32)
            raw[r * channels : (r + 1) * channels, :] = (
                land[r : r + 1, :] * (own[r].astype(f32) + update)
            ).astype(bf16)
        polar_filter(raw, keep, polar, table, out, select)


def scratch(rows, channels, width, hid):
    return [
        pltpu.VMEM((rows, channels, width), f32),
        pltpu.VMEM((channels + BIAS_ROWS, width), bf16),
        pltpu.VMEM((hid, width), f32),
        pltpu.VMEM((hid, width), bf16),
        pltpu.VMEM((rows * channels, width), bf16),
    ]


SMEM = pl.BlockSpec(memory_space=pltpu.SMEM)
VMEM = pl.BlockSpec(memory_space=pltpu.VMEM)
LIMIT = 24 << 20


def per_device(
    states, land_mask, cutoff, kernel, norm_gain, norm_bias, weight_in, bias_in, weight_out
):
    member = states[0]
    rows, channels, width = member.shape
    hid = weight_in.shape[1]
    bands = lax.axis_size("lat")
    members = lax.axis_size("mem")
    total_rows = rows * bands
    me = lax.axis_index("mem")
    select = total_rows > 2 * POLAR
    field = jax.ShapeDtypeStruct((rows, channels, width), bf16)
    params = pltpu.CompilerParams(vmem_limit_bytes=LIMIT)

    def send(block, pairs):
        return lax.ppermute(block, ("mem", "lat"), [(a * bands + i, b * bands + j) for (a, i), (b, j) in pairs])

    def exchange(block, which):
        forward = [((m, z), (m, z + 1)) for m in which for z in range(bands - 1)]
        return send(block, forward), send(block, [(b, a) for a, b in forward])

    def across(block, pairs):
        return send(block, [((a, z), (b, z)) for a, b in pairs for z in range(bands)])

    evens = list(range(0, members, 2))
    partners = [(m, m + 1) for m in evens if m + 1 < members]
    odd = me % 2 == 1

    up, down = exchange(member, range(members))
    control = member
    count = 2
    while count < members:
        sent = across(control, [(m, m + count) for m in range(0, count, 2) if m + count < members])
        control = jnp.where((me >= count) & (me < 2 * count), sent, control)
        count *= 2
    control_up, control_down = exchange(control, evens[1:])
    control_up = jnp.where(me == 0, up, control_up)
    control_down = jnp.where(me == 0, down, control_down)
    control = jnp.where(odd, across(control, partners), control)

    table, wavenumber = fourier(width)
    table = jnp.asarray(table)
    row = lax.axis_index("lat") * rows + jnp.arange(rows)
    is_polar = (row < POLAR) | (row >= total_rows - POLAR)
    place = jnp.clip(jnp.where(row < POLAR, row, row - total_rows + 2 * POLAR), 0, 2 * POLAR - 1)
    keep = (jnp.asarray(wavenumber)[None, :] <= cutoff[place][:, None]).astype(f32)
    flags = jnp.concatenate([is_polar.astype(jnp.int32), (me == 0).astype(jnp.int32)[None]])
    land = land_mask.astype(f32)
    high = lax.reduce_precision(bias_in, 8, 7)
    middle = lax.reduce_precision(bias_in - high, 8, 7)
    low = bias_in - high - middle
    bias_rows = jnp.pad(jnp.stack([high, middle, low]), ((0, BIAS_ROWS - 3), (0, 0))).astype(bf16)
    w_in = jnp.concatenate([weight_in, bias_rows], axis=0).T
    w_out = weight_out.T
    taps, gain, offset = pl.pallas_call(
        prepare_kernel,
        out_shape=(
            jax.ShapeDtypeStruct((rows, TAPS, channels, (rows + 2 * HALO) * GROUP), bf16),
            jax.ShapeDtypeStruct((channels, LANES), f32),
            jax.ShapeDtypeStruct((channels, LANES), f32),
        ),
        in_specs=[VMEM] * 3,
        out_specs=(VMEM,) * 3,
        compiler_params=params,
        name="prepare",
    )(kernel.transpose(1, 2, 0), norm_gain[:, None], norm_bias[:, None])

    def control_step(up, own, down):
        return pl.pallas_call(
            lambda *refs: control_kernel(select, True, *refs),
            out_shape=(
                field,
                jax.ShapeDtypeStruct((rows, channels, width), f32),
                jax.ShapeDtypeStruct((rows, 1, width), f32),
                jax.ShapeDtypeStruct((rows, hid, width), f32),
            ),
            in_specs=[SMEM] + [VMEM] * 11,
            out_specs=(VMEM,) * 4,
            scratch_shapes=scratch(rows, channels, width, hid),
            compiler_params=params,
            name="control",
        )(flags, up, own, down, taps, gain, offset, w_in, w_out, land, keep, table)

    def tangent_step(up, own, down, unit, scale, slope, advanced):
        return pl.pallas_call(
            lambda *refs: tangent_kernel(select, *refs),
            out_shape=field,
            in_specs=[SMEM] + [VMEM] * 14,
            out_specs=VMEM,
            scratch_shapes=scratch(rows, channels, width, hid),
            compiler_params=params,
            name="tangent",
        )(flags, up, own, down, taps, gain, w_in, w_out, land, keep, table, unit, scale, slope, advanced)

    for step in range(STEPS):
        if step > 0:
            up, down = exchange(member, range(1, members))
            control_up, control_down, _ = lax.optimization_barrier((control_up, control_down, member))
        control_up = jnp.where(odd, across(control_up, partners), control_up)
        control_down = jnp.where(odd, across(control_down, partners), control_down)
        control, unit, scale, slope = control_step(control_up, control, control_down)
        if step + 1 < STEPS:
            control_up, control_down = exchange(control, evens)
        member = tangent_step(up, member, down, unit, scale, slope, control)
    return member[None]


def solution(mesh):
    in_specs = (
        P(("runs", "mem"), "lat", None, None),
        P("lat", None),
        P(),
        P(),
        P(),
        P(),
        P(),
        P(),
        P(),
    )
    out_specs = P(("runs", "mem"), "lat", None, None)
    return jax.shard_map(
        per_device, mesh=mesh, in_specs=in_specs, out_specs=out_specs, check_vma=False
    )
```

```python
import math

import jax
import jax.numpy as jnp
import numpy as np
from jax import lax
from jax.experimental import pallas as pl
from jax.experimental.pallas import tpu as pltpu
from jax.sharding import PartitionSpec as P

STEPS = 2
POLAR = 6
HALO = 3
TAPS = 7
GROUP = 16
LANES = 256
CHUNK = 64
BIAS_ROWS = 16
SPARE = 8

gelu_scale = 0.7978845608028654
gelu_cubic = 0.044715
epsilon = 1e-05

f32 = jnp.float32
bf16 = jnp.bfloat16


def fourier(width):
    index = np.arange(width, dtype=np.int32)
    wavenumber = np.where(index <= width // 2, index, index - width // 2).astype(np.int32)
    phase = index[:, None] * wavenumber[None, :] % width
    angle = phase.astype(np.float64) * (2.0 * math.pi / width)
    factor = np.where((index == 0) | (index == width // 2), 1.0 / math.sqrt(width), math.sqrt(2.0 / width))
    table = np.where(index[None, :] <= width // 2, np.cos(angle), np.sin(angle)) * factor[None, :]
    return table.astype(np.float32).astype(bf16)


def unroll(count, most):
    return max(u for u in range(1, most + 1) if count % u == 0)


def prepare_kernel(*refs):
    sources, refs = refs[:6], refs[6:]
    taps, gain_out, offset_out, w_in, land = refs[:5]
    kernel, gain, offset, weight_in, bias, land_mask, arrived = refs[5:]
    copies = [
        pltpu.make_async_copy(source, here, arrived.at[i])
        for i, (source, here) in enumerate(zip(sources, (kernel, gain, offset, weight_in, bias, land_mask)))
    ]
    for copy in copies:
        copy.start()
    for copy in copies:
        copy.wait()
    rows, _, channels, depth = taps.shape
    band = lax.axis_index("lat")
    lane = lax.broadcasted_iota(jnp.int32, (channels, depth), 1)
    here = lax.broadcasted_iota(jnp.int32, (channels, depth), 0)
    block = lane // GROUP
    turned = jnp.where(block < HALO, block + rows + HALO, jnp.where(block < HALO + rows, block, block - rows - HALO))
    block = jnp.where(band % 2 == 1, block, turned)
    block = jnp.where(lane % GROUP == here % GROUP, block, -1)
    for j in range(TAPS):
        lines = [kernel[i, j : j + 1, :] for i in range(TAPS)] + [jnp.zeros((128 - TAPS, channels), f32)]
        turned = jnp.concatenate(lines, axis=0).T
        columns = [jnp.broadcast_to(turned[:, i : i + 1], (channels, depth)) for i in range(TAPS)]
        for r in range(rows):
            total = jnp.zeros((channels, depth), f32)
            for i in range(TAPS):
                total = jnp.where(block == r + i, columns[i], total)
            taps[r, j] = total.astype(bf16)
    gain_out[...] = jnp.broadcast_to(gain[...], (128, channels)).T
    offset_out[...] = jnp.broadcast_to(offset[...], (128, channels)).T
    w_in[:, :channels] = weight_in[...].astype(f32).T.astype(bf16)
    place = lax.broadcasted_iota(jnp.int32, (128, 128), 1)
    for k in range(bias.shape[0]):
        value = jnp.broadcast_to(bias[k : k + 1, :], (128, 128)).T
        high = value.astype(bf16).astype(f32)
        middle = (value - high).astype(bf16).astype(f32)
        low = value - high - middle
        three = jnp.where(place == 0, high, jnp.where(place == 1, middle, jnp.where(place == 2, low, 0.0)))
        w_in[k * 128 : (k + 1) * 128, channels:] = three[:, :BIAS_ROWS].astype(bf16)
    land[...] = land_mask[...].astype(f32)


def filter_kernel(bands, cutoff, table, out):
    rows, width, _ = out.shape
    band = lax.axis_index("lat")
    index = lax.broadcasted_iota(jnp.int32, (1, width), 1)
    wavenumber = jnp.where(index <= width // 2, index, index - width // 2)
    total_rows = rows * bands
    for r in range(rows):
        row = band * rows + r
        place = jnp.clip(jnp.where(row < POLAR, row, row - total_rows + 2 * POLAR), 0, 2 * POLAR - 1)
        kept = (table[...].astype(f32) * (wavenumber <= cutoff[place]).astype(f32)).astype(bf16)
        out[r] = lax.dot_general(
            kept, table[...], (((1,), (1,)), ((), ())), preferred_element_type=f32
        ).astype(bf16)
        if total_rows > 2 * POLAR:
            @pl.when((row >= POLAR) & (row < total_rows - POLAR))
            def _():
                across = lax.broadcasted_iota(jnp.int32, (width, width), 1)
                along = lax.broadcasted_iota(jnp.int32, (width, width), 0)
                out[r] = (across == along).astype(f32).astype(bf16)


def convolve(near, own, far, taps, out):
    rows, channels, width = out.shape

    def group(b, _):
        at = pl.ds(pl.multiple_of(b * GROUP, GROUP), GROUP)
        field = jnp.concatenate([near(at), own(at), far(at)], axis=0)
        field = field.reshape((rows + 2 * HALO) * GROUP, width)
        parts = jnp.dot(taps[:, :, at, :].reshape(rows * TAPS * GROUP, field.shape[0]), field, preferred_element_type=f32)
        for r in range(rows):
            part = [parts[(r * TAPS + j) * GROUP : (r * TAPS + j + 1) * GROUP] for j in range(TAPS)]
            total = part[HALO]
            for j in range(TAPS):
                if j != HALO:
                    total = total + pltpu.roll(part[j], (HALO - j) % width, 1)
            out[r, at, :] = total
        return 0

    groups = channels // GROUP
    lax.fori_loop(0, groups, group, 0, unroll=unroll(groups, 5))


def read(ref):
    return lambda at: ref[:, at, :]


def choose(second, first, other):
    if other is None:
        return read(first)
    return lambda at: jnp.where(second, other[:, at, :], first[:, at, :])


def pipeline(tiles, first, second, third):
    for i in range(tiles + 2):
        if i < tiles:
            first(i)
        if 1 <= i <= tiles:
            second(i - 1)
        if i >= 2:
            third(i - 2)


def add_bias_rows(normed, channels):
    row = lax.broadcasted_iota(jnp.int32, (BIAS_ROWS, normed.shape[1]), 0)
    normed[channels:, :] = jnp.where(row < 3, 1.0, 0.0).astype(bf16)


def polar_filter(raw, filters, out, r):
    channels = raw.shape[0] // filters.shape[0]
    out[r, :channels, :] = jnp.dot(
        raw[r * channels : (r + 1) * channels, :], filters[r], preferred_element_type=f32
    ).astype(bf16)


def control_kernel(swap, *refs):
    near, own, far = refs[:3]
    refs = refs[3:]
    if swap:
        other = [far, None, near]
    else:
        other, refs = refs[:3], refs[3:]
    (
        taps, gain, bias, w_in, w_out, land, filters,
        out, unit_out, scale_out, slope_out, conv, normed, normed_b, hidden, hidden_b, act, act_b, raw,
    ) = refs
    rows, channels, width = out.shape
    hid = w_in.shape[0]
    normed, hidden, act = (normed, normed_b), (hidden, hidden_b), (act, act_b)
    second = lax.axis_index("mem") % 2 == 1
    for block in normed:
        add_bias_rows(block, channels)
    convolve(*(choose(second, a, b) for a, b in zip((near, own, far), other)), taps, conv)
    across = width // LANES

    def place(i):
        return i // across, slice(i % across * LANES, (i % across + 1) * LANES)

    def first(i):
        r, at = place(i)
        for w in range(0, LANES, 128):
            here, there = slice(at.start + w, at.start + w + 128), slice(w, w + 128)
            value = conv[r, :, here]
            centered = value - jnp.mean(value, axis=0, keepdims=True)
            scale = lax.rsqrt(jnp.mean(centered * centered, axis=0, keepdims=True) + epsilon)
            unit = centered * scale
            unit_out[r, :, here] = unit
            scale_out[r, :, here] = scale
            normed[i % 2][:channels, there] = (unit * gain[...] + bias[...]).astype(bf16)
        hidden[i % 2][...] = jnp.dot(w_in[...], normed[i % 2][...], preferred_element_type=f32)

    def pair(i):
        r, at = place(i)
        for c in range(0, hid, CHUNK):
            h = hidden[i % 2][c : c + CHUNK, :]
            square = h * h
            t = jnp.tanh(h * (gelu_scale + (gelu_scale * gelu_cubic) * square))
            half = 0.5 + 0.5 * t
            act[i % 2][c : c + CHUNK, :] = (h * half).astype(bf16)
            lean = h * (2.0 * gelu_scale + (6.0 * gelu_scale * gelu_cubic) * square)
            slope_out[r, c : c + CHUNK, at] = half * (1.0 + (1.0 - half) * lean)

    def third(i):
        r, at = place(i)
        update = jnp.dot(w_out[...], act[i % 2][...], preferred_element_type=f32)
        field = own[r, :, at]
        if other[1] is not None:
            field = jnp.where(second, other[1][r, :, at], field)
        raw[r * channels : (r + 1) * channels, at] = (land[r : r + 1, at] * (field.astype(f32) + update)).astype(bf16)
        if i % across == across - 1:
            polar_filter(raw, filters, out, r)

    pipeline(rows * across, first, pair, third)


def conv_kernel(near, own, far, taps, out):
    convolve(read(near), read(own), read(far), taps, out)


def tangent_kernel(ready, *refs):
    if ready:
        own, conv = refs[:2]
        refs = refs[2:]
    else:
        near, own, far, taps = refs[:4]
        refs = refs[4:]
    gain, w_in, w_out, land, filters, unit_in, scale_in, slope_in, advanced, out = refs[:10]
    refs = refs[10:]
    if not ready:
        conv, refs = refs[0], refs[1:]
    normed, normed_b, hidden, hidden_b, act, act_b, raw = refs
    normed, hidden, act = (normed, normed_b), (hidden, hidden_b), (act, act_b)
    rows, channels, width = advanced.shape
    hid = w_in.shape[0]
    across = width // LANES
    is_control = lax.axis_index("mem") == 0

    def place(i):
        return i // across, slice(i % across * LANES, (i % across + 1) * LANES)

    def first(i):
        r, at = place(i)
        for w in range(0, LANES, 128):
            here, there = slice(at.start + w, at.start + w + 128), slice(w, w + 128)
            value = conv[r, :, here]
            unit = unit_in[r, :, here]
            average = jnp.mean(value, axis=0, keepdims=True)
            along = jnp.mean(value * unit, axis=0, keepdims=True)
            normed[i % 2][:, there] = (gain[...] * scale_in[r, :, here] * (value - average - unit * along)).astype(bf16)
        hidden[i % 2][...] = jnp.dot(w_in[:, :channels], normed[i % 2][...], preferred_element_type=f32)

    def mix(i):
        r, at = place(i)
        for c in range(0, hid, CHUNK):
            act[i % 2][c : c + CHUNK, :] = (slope_in[r, c : c + CHUNK, at] * hidden[i % 2][c : c + CHUNK, :]).astype(bf16)

    def third(i):
        r, at = place(i)
        update = jnp.dot(w_out[...], act[i % 2][...], preferred_element_type=f32)
        raw[r * channels : (r + 1) * channels, at] = (
            land[r : r + 1, at] * (own[r, :channels, at].astype(f32) + update)
        ).astype(bf16)
        if i % across == across - 1:
            polar_filter(raw, filters, out, r)

    if out.shape[1] > channels:
        out[:, channels:, :] = jnp.zeros((rows, out.shape[1] - channels, width), bf16)

    @pl.when(is_control)
    def _():
        out[:, :channels, :] = advanced[...]

    @pl.when(jnp.logical_not(is_control))
    def _():
        if not ready:
            convolve(read(near), read(own), read(far), taps, conv)
        pipeline(rows * across, first, mix, third)


def scratch(rows, channels, width, hid, bias_rows, conv=True):
    return ([pltpu.VMEM((rows, channels, width), f32)] if conv else []) + [
        pltpu.VMEM((channels + bias_rows, LANES), bf16),
        pltpu.VMEM((channels + bias_rows, LANES), bf16),
        pltpu.VMEM((hid, LANES), f32),
        pltpu.VMEM((hid, LANES), f32),
        pltpu.VMEM((hid, LANES), bf16),
        pltpu.VMEM((hid, LANES), bf16),
        pltpu.VMEM((rows * channels, width), bf16),
    ]


SMEM = pl.BlockSpec(memory_space=pltpu.SMEM)
VMEM = pl.BlockSpec(memory_space=pltpu.VMEM)
LIMIT = 24 << 20


def per_device(
    states, land_mask, cutoff, kernel, norm_gain, norm_bias, weight_in, bias_in, weight_out
):
    member = states[0]
    rows, channels, width = member.shape
    hid = weight_in.shape[1]
    bands = lax.axis_size("lat")
    members = lax.axis_size("mem")
    me = lax.axis_index("mem")
    params = pltpu.CompilerParams(vmem_limit_bytes=LIMIT)

    def shape(*dims, kind=f32):
        return jax.ShapeDtypeStruct(dims, kind)

    field = shape(rows, channels, width, kind=bf16)

    def send(block, pairs):
        return lax.ppermute(block, ("mem", "lat"), [(a * bands + i, b * bands + j) for (a, i), (b, j) in pairs])

    def neighbours(which, start):
        pairs = [((m, z), (m, z + 1)) for m in which for z in range(start, bands - 1, 2)]
        return pairs + [(b, a) for a, b in pairs]

    def exchange(block, which):
        far = send(block, neighbours(which, 1))
        return send(block, neighbours(which, 0)), far

    def across(block, pairs):
        return send(block, [((a, z), (b, z)) for a, b in pairs for z in range(bands)])

    evens = list(range(0, members, 2))
    odds = list(range(1, members, 2))
    partners = [(m - 1, m) for m in odds]
    swapped = partners + [(b, a) for a, b in partners]

    table = jnp.asarray(fourier(width))
    w_out = weight_out.T
    sources = (kernel, norm_gain[None], norm_bias[None], weight_in, bias_in.reshape(-1, 128), land_mask)
    taps, gain, offset, w_in, land = pl.pallas_call(
        prepare_kernel,
        out_shape=(
            shape(rows, TAPS, channels, (rows + 2 * HALO) * GROUP, kind=bf16),
            shape(channels, 128),
            shape(channels, 128),
            shape(hid, channels + BIAS_ROWS, kind=bf16),
            shape(rows, width),
        ),
        in_specs=[pl.BlockSpec(memory_space=pltpu.MemorySpace.HBM)] * 6,
        out_specs=(VMEM,) * 5,
        scratch_shapes=[pltpu.VMEM(x.shape, x.dtype) for x in sources] + [pltpu.SemaphoreType.DMA((6,))],
        compiler_params=params,
        name="prepare",
    )(*sources)
    filters = pl.pallas_call(
        lambda *refs: filter_kernel(bands, *refs),
        out_shape=shape(rows, width, width, kind=bf16),
        in_specs=[SMEM, VMEM],
        out_specs=VMEM,
        compiler_params=params,
        name="filters",
    )(cutoff, table)

    def control_step(*halos):
        return pl.pallas_call(
            lambda *refs: control_kernel(len(halos) == 3, *refs),
            out_shape=(field, shape(rows, channels, width), shape(rows, 1, width), shape(rows, hid, width)),
            in_specs=[VMEM] * (7 + len(halos)),
            out_specs=(VMEM,) * 4,
            scratch_shapes=scratch(rows, channels, width, hid, BIAS_ROWS),
            compiler_params=params,
            name="control",
        )(*halos, taps, gain, offset, w_in, w_out, land, filters)

    def conv_step(near, own, far):
        return pl.pallas_call(
            conv_kernel,
            out_shape=shape(rows, channels, width),
            in_specs=[VMEM] * 4,
            out_specs=VMEM,
            compiler_params=params,
            name="conv",
        )(near, own, far, taps)

    def tangent_step(ready, spare, inputs, unit, scale, slope, advanced):
        return pl.pallas_call(
            lambda *refs: tangent_kernel(ready, *refs),
            out_shape=shape(rows, channels + spare, width, kind=bf16),
            in_specs=[VMEM] * (9 + len(inputs)),
            out_specs=VMEM,
            scratch_shapes=scratch(rows, channels, width, hid, 0, not ready),
            compiler_params=params,
            name="tangent",
        )(*inputs, gain, w_in, w_out, land, filters, unit, scale, slope, advanced)

    near, far = exchange(member, range(1, members))
    control = member
    count = 2
    while count < members:
        sent = across(control, [(m, m + count) for m in range(0, count, 2) if m + count < members])
        control = jnp.where((me >= count) & (me < 2 * count), sent, control)
        count *= 2
    control, taps = lax.optimization_barrier((control, taps))
    control_other = across(control, partners)
    control_near, control_far = exchange(control, evens)
    conv = conv_step(near, member, far)
    control_near, control_far, conv, filters = lax.optimization_barrier((control_near, control_far, conv, filters))
    other = (across(control_near, partners), control_other, across(control_far, partners))
    control, unit, scale, slope = control_step(control_near, control, control_far, *other)
    for step in range(1, STEPS):
        halo = send(control, neighbours(evens, 0) + neighbours(odds, 1))
        inputs = (member, conv) if step == 1 else (near, member, far, taps)
        member = tangent_step(step == 1, SPARE, inputs, unit, scale, slope, control)
        halo, _ = lax.optimization_barrier((halo, member))
        other = across(halo, swapped)
        near, far = exchange(member, range(1, members))
        control, unit, scale, slope = control_step(halo, control, other)
    return tangent_step(False, 0, (near, member, far, taps), unit, scale, slope, control)[None]


def solution(mesh):
    in_specs = (
        P(("runs", "mem"), "lat", None, None),
        P("lat", None),
        P(),
        P(),
        P(),
        P(),
        P(),
        P(),
        P(),
    )
    out_specs = P(("runs", "mem"), "lat", None, None)
    return jax.shard_map(
        per_device, mesh=mesh, in_specs=in_specs, out_specs=out_specs, check_vma=False
    )
```

```python
import math

import jax
import jax.numpy as jnp
import numpy as np
from jax import lax
from jax.experimental import pallas as pl
from jax.experimental.pallas import tpu as pltpu
from jax.sharding import PartitionSpec as P

STEPS = 2
POLAR = 6
HALO = 3
TAPS = 7
GROUP = 16
LANES = 256
CHUNK = 64
BIAS_ROWS = 16
SPARE = 8

gelu_scale = 0.7978845608028654
gelu_cubic = 0.044715
epsilon = 1e-05

f32 = jnp.float32
bf16 = jnp.bfloat16


def fourier(width):
    index = np.arange(width, dtype=np.int32)
    wavenumber = np.where(index <= width // 2, index, index - width // 2).astype(np.int32)
    phase = index[:, None] * wavenumber[None, :] % width
    angle = phase.astype(np.float64) * (2.0 * math.pi / width)
    factor = np.where((index == 0) | (index == width // 2), 1.0 / math.sqrt(width), math.sqrt(2.0 / width))
    table = np.where(index[None, :] <= width // 2, np.cos(angle), np.sin(angle)) * factor[None, :]
    return table.astype(np.float32).astype(bf16)


def unroll(count, most):
    return max(u for u in range(1, most + 1) if count % u == 0)


def prepare_kernel(*refs):
    sources, refs = refs[:6], refs[6:]
    taps, gain_out, offset_out, w_in, land = refs[:5]
    kernel, gain, offset, weight_in, bias, land_mask, arrived = refs[5:]
    copies = [
        pltpu.make_async_copy(source, here, arrived.at[i])
        for i, (source, here) in enumerate(zip(sources, (kernel, gain, offset, weight_in, bias, land_mask)))
    ]
    for copy in copies:
        copy.start()
    for copy in copies:
        copy.wait()
    rows, _, channels, depth = taps.shape
    band = lax.axis_index("lat")
    lane = lax.broadcasted_iota(jnp.int32, (channels, depth), 1)
    here = lax.broadcasted_iota(jnp.int32, (channels, depth), 0)
    block = lane // GROUP
    turned = jnp.where(block < HALO, block + rows + HALO, jnp.where(block < HALO + rows, block, block - rows - HALO))
    block = jnp.where((band + lax.axis_index("mem")) % 2 == 1, block, turned)
    block = jnp.where(lane % GROUP == here % GROUP, block, -1)
    for j in range(TAPS):
        lines = [kernel[i, j : j + 1, :] for i in range(TAPS)] + [jnp.zeros((128 - TAPS, channels), f32)]
        turned = jnp.concatenate(lines, axis=0).T
        columns = [jnp.broadcast_to(turned[:, i : i + 1], (channels, depth)) for i in range(TAPS)]
        for r in range(rows):
            total = jnp.zeros((channels, depth), f32)
            for i in range(TAPS):
                total = jnp.where(block == r + i, columns[i], total)
            taps[r, j] = total.astype(bf16)
    gain_out[...] = jnp.broadcast_to(gain[...], (128, channels)).T
    offset_out[...] = jnp.broadcast_to(offset[...], (128, channels)).T
    w_in[:, :channels] = weight_in[...].astype(f32).T.astype(bf16)
    place = lax.broadcasted_iota(jnp.int32, (128, 128), 1)
    for k in range(bias.shape[0]):
        value = jnp.broadcast_to(bias[k : k + 1, :], (128, 128)).T
        high = value.astype(bf16).astype(f32)
        middle = (value - high).astype(bf16).astype(f32)
        low = value - high - middle
        three = jnp.where(place == 0, high, jnp.where(place == 1, middle, jnp.where(place == 2, low, 0.0)))
        w_in[k * 128 : (k + 1) * 128, channels:] = three[:, :BIAS_ROWS].astype(bf16)
    land[...] = land_mask[...].astype(f32)


def filter_kernel(bands, cutoff, table, out):
    rows, width, _ = out.shape
    band = lax.axis_index("lat")
    index = lax.broadcasted_iota(jnp.int32, (1, width), 1)
    wavenumber = jnp.where(index <= width // 2, index, index - width // 2)
    total_rows = rows * bands
    for r in range(rows):
        row = band * rows + r
        place = jnp.clip(jnp.where(row < POLAR, row, row - total_rows + 2 * POLAR), 0, 2 * POLAR - 1)
        kept = (table[...].astype(f32) * (wavenumber <= cutoff[place]).astype(f32)).astype(bf16)
        out[r] = lax.dot_general(
            kept, table[...], (((1,), (1,)), ((), ())), preferred_element_type=f32
        ).astype(bf16)
        if total_rows > 2 * POLAR:
            @pl.when((row >= POLAR) & (row < total_rows - POLAR))
            def _():
                across = lax.broadcasted_iota(jnp.int32, (width, width), 1)
                along = lax.broadcasted_iota(jnp.int32, (width, width), 0)
                out[r] = (across == along).astype(f32).astype(bf16)


def convolve(near, own, far, taps, out):
    rows, channels, width = out.shape

    def group(b, _):
        at = pl.ds(pl.multiple_of(b * GROUP, GROUP), GROUP)
        field = jnp.concatenate([near(at), own(at), far(at)], axis=0)
        field = field.reshape((rows + 2 * HALO) * GROUP, width)
        parts = jnp.dot(taps[:, :, at, :].reshape(rows * TAPS * GROUP, field.shape[0]), field, preferred_element_type=f32)
        for r in range(rows):
            part = [parts[(r * TAPS + j) * GROUP : (r * TAPS + j + 1) * GROUP] for j in range(TAPS)]
            total = part[HALO]
            for j in range(TAPS):
                if j != HALO:
                    total = total + pltpu.roll(part[j], (HALO - j) % width, 1)
            out[r, at, :] = total
        return 0

    groups = channels // GROUP
    lax.fori_loop(0, groups, group, 0, unroll=unroll(groups, 5))


def read(ref):
    return lambda at: ref[:, at, :]


def choose(odd, first, other):
    return lambda at: jnp.where(odd, other[:, at, :], first[:, at, :])


def pipeline(tiles, first, second, third):
    for i in range(tiles + 2):
        if i < tiles:
            first(i)
        if 1 <= i <= tiles:
            second(i - 1)
        if i >= 2:
            third(i - 2)


def add_bias_rows(normed, channels):
    row = lax.broadcasted_iota(jnp.int32, (BIAS_ROWS, normed.shape[1]), 0)
    normed[channels:, :] = jnp.where(row < 3, 1.0, 0.0).astype(bf16)


def polar_filter(raw, filters, out, r):
    channels = raw.shape[0] // filters.shape[0]
    out[r, :channels, :] = jnp.dot(
        raw[r * channels : (r + 1) * channels, :], filters[r], preferred_element_type=f32
    ).astype(bf16)


def control_kernel(*refs):
    first_halo, own, second_halo = refs[:3]
    refs = refs[3:]
    other = None
    if len(refs) > 19:
        other, refs = refs[:3], refs[3:]
    (
        taps, gain, bias, w_in, w_out, land, filters,
        out, unit_out, scale_out, slope_out, conv, normed, normed_b, hidden, hidden_b, act, act_b, raw,
    ) = refs
    rows, channels, width = out.shape
    hid = w_in.shape[0]
    normed, hidden, act = (normed, normed_b), (hidden, hidden_b), (act, act_b)
    odd = lax.axis_index("mem") % 2 == 1
    for block in normed:
        add_bias_rows(block, channels)
    blocks = [read(first_halo), read(own), read(second_halo)]
    if other is not None:
        blocks = [choose(odd, a, b) for a, b in zip((first_halo, own, second_halo), other)]
    convolve(*blocks, taps, conv)
    across = width // LANES

    def place(i):
        return i // across, slice(i % across * LANES, (i % across + 1) * LANES)

    def first(i):
        r, at = place(i)
        for w in range(0, LANES, 128):
            here, there = slice(at.start + w, at.start + w + 128), slice(w, w + 128)
            value = conv[r, :, here]
            centered = value - jnp.mean(value, axis=0, keepdims=True)
            scale = lax.rsqrt(jnp.mean(centered * centered, axis=0, keepdims=True) + epsilon)
            unit = centered * scale
            unit_out[r, :, here] = unit
            scale_out[r, :, here] = scale
            normed[i % 2][:channels, there] = (unit * gain[...] + bias[...]).astype(bf16)
        hidden[i % 2][...] = jnp.dot(w_in[...], normed[i % 2][...], preferred_element_type=f32)

    def pair(i):
        r, at = place(i)
        for c in range(0, hid, CHUNK):
            h = hidden[i % 2][c : c + CHUNK, :]
            square = h * h
            t = jnp.tanh(h * (gelu_scale + (gelu_scale * gelu_cubic) * square))
            half = 0.5 + 0.5 * t
            act[i % 2][c : c + CHUNK, :] = (h * half).astype(bf16)
            lean = h * (2.0 * gelu_scale + (6.0 * gelu_scale * gelu_cubic) * square)
            slope_out[r, c : c + CHUNK, at] = half * (1.0 + (1.0 - half) * lean)

    def third(i):
        r, at = place(i)
        update = jnp.dot(w_out[...], act[i % 2][...], preferred_element_type=f32)
        field = own[r, :, at]
        if other is not None:
            field = jnp.where(odd, other[1][r, :, at], field)
        raw[r * channels : (r + 1) * channels, at] = (land[r : r + 1, at] * (field.astype(f32) + update)).astype(bf16)
        if i % across == across - 1:
            polar_filter(raw, filters, out, r)

    pipeline(rows * across, first, pair, third)


def conv_kernel(near, own, far, taps, out):
    convolve(read(near), read(own), read(far), taps, out)


def tangent_kernel(ready, *refs):
    if ready:
        own, conv = refs[:2]
        refs = refs[2:]
    else:
        near, own, far, taps = refs[:4]
        refs = refs[4:]
    gain, w_in, w_out, land, filters, unit_in, scale_in, slope_in, advanced, out = refs[:10]
    refs = refs[10:]
    if not ready:
        conv, refs = refs[0], refs[1:]
    normed, normed_b, hidden, hidden_b, act, act_b, raw = refs
    normed, hidden, act = (normed, normed_b), (hidden, hidden_b), (act, act_b)
    rows, channels, width = advanced.shape
    hid = w_in.shape[0]
    across = width // LANES
    is_control = lax.axis_index("mem") == 0

    def place(i):
        return i // across, slice(i % across * LANES, (i % across + 1) * LANES)

    def first(i):
        r, at = place(i)
        for w in range(0, LANES, 128):
            here, there = slice(at.start + w, at.start + w + 128), slice(w, w + 128)
            value = conv[r, :, here]
            unit = unit_in[r, :, here]
            average = jnp.mean(value, axis=0, keepdims=True)
            along = jnp.mean(value * unit, axis=0, keepdims=True)
            normed[i % 2][:, there] = (gain[...] * scale_in[r, :, here] * (value - average - unit * along)).astype(bf16)
        hidden[i % 2][...] = jnp.dot(w_in[:, :channels], normed[i % 2][...], preferred_element_type=f32)

    def mix(i):
        r, at = place(i)
        for c in range(0, hid, CHUNK):
            act[i % 2][c : c + CHUNK, :] = (slope_in[r, c : c + CHUNK, at] * hidden[i % 2][c : c + CHUNK, :]).astype(bf16)

    def third(i):
        r, at = place(i)
        update = jnp.dot(w_out[...], act[i % 2][...], preferred_element_type=f32)
        raw[r * channels : (r + 1) * channels, at] = (
            land[r : r + 1, at] * (own[r, :channels, at].astype(f32) + update)
        ).astype(bf16)
        if i % across == across - 1:
            polar_filter(raw, filters, out, r)

    if out.shape[1] > channels:
        out[:, channels:, :] = jnp.zeros((rows, out.shape[1] - channels, width), bf16)

    @pl.when(is_control)
    def _():
        out[:, :channels, :] = advanced[...]

    @pl.when(jnp.logical_not(is_control))
    def _():
        if not ready:
            convolve(read(near), read(own), read(far), taps, conv)
        pipeline(rows * across, first, mix, third)


def scratch(rows, channels, width, hid, bias_rows, conv=True):
    return ([pltpu.VMEM((rows, channels, width), f32)] if conv else []) + [
        pltpu.VMEM((channels + bias_rows, LANES), bf16),
        pltpu.VMEM((channels + bias_rows, LANES), bf16),
        pltpu.VMEM((hid, LANES), f32),
        pltpu.VMEM((hid, LANES), f32),
        pltpu.VMEM((hid, LANES), bf16),
        pltpu.VMEM((hid, LANES), bf16),
        pltpu.VMEM((rows * channels, width), bf16),
    ]


SMEM = pl.BlockSpec(memory_space=pltpu.SMEM)
VMEM = pl.BlockSpec(memory_space=pltpu.VMEM)
LIMIT = 24 << 20


def per_device(
    states, land_mask, cutoff, kernel, norm_gain, norm_bias, weight_in, bias_in, weight_out
):
    member = states[0]
    rows, channels, width = member.shape
    hid = weight_in.shape[1]
    bands = lax.axis_size("lat")
    members = lax.axis_size("mem")
    me = lax.axis_index("mem")
    params = pltpu.CompilerParams(vmem_limit_bytes=LIMIT)

    def shape(*dims, kind=f32):
        return jax.ShapeDtypeStruct(dims, kind)

    field = shape(rows, channels, width, kind=bf16)

    def send(block, pairs):
        return lax.ppermute(block, ("mem", "lat"), [(a * bands + i, b * bands + j) for (a, i), (b, j) in pairs])

    def neighbours(which, start):
        pairs = [((m, z), (m, z + 1)) for m in which for z in range(start, bands - 1, 2)]
        return pairs + [(b, a) for a, b in pairs]

    def exchange(block, which):
        even, odd = [m for m in which if m % 2 == 0], [m for m in which if m % 2 == 1]
        first = send(block, neighbours(even, 0) + neighbours(odd, 1))
        return first, send(block, neighbours(even, 1) + neighbours(odd, 0))

    def across(block, pairs):
        return send(block, [((a, z), (b, z)) for a, b in pairs for z in range(bands)])

    evens = list(range(0, members, 2))
    odds = list(range(1, members, 2))
    partners = [(m - 1, m) for m in odds]
    swapped = partners + [(b, a) for a, b in partners]

    table = jnp.asarray(fourier(width))
    w_out = weight_out.T
    sources = (kernel, norm_gain[None], norm_bias[None], weight_in, bias_in.reshape(-1, 128), land_mask)
    taps, gain, offset, w_in, land = pl.pallas_call(
        prepare_kernel,
        out_shape=(
            shape(rows, TAPS, channels, (rows + 2 * HALO) * GROUP, kind=bf16),
            shape(channels, 128),
            shape(channels, 128),
            shape(hid, channels + BIAS_ROWS, kind=bf16),
            shape(rows, width),
        ),
        in_specs=[pl.BlockSpec(memory_space=pltpu.MemorySpace.HBM)] * 6,
        out_specs=(VMEM,) * 5,
        scratch_shapes=[pltpu.VMEM(x.shape, x.dtype) for x in sources] + [pltpu.SemaphoreType.DMA((6,))],
        compiler_params=params,
        name="prepare",
    )(*sources)
    filters = pl.pallas_call(
        lambda *refs: filter_kernel(bands, *refs),
        out_shape=shape(rows, width, width, kind=bf16),
        in_specs=[SMEM, VMEM],
        out_specs=VMEM,
        compiler_params=params,
        name="filters",
    )(cutoff, table)

    def control_step(*halos):
        return pl.pallas_call(
            control_kernel,
            out_shape=(field, shape(rows, channels, width), shape(rows, 1, width), shape(rows, hid, width)),
            in_specs=[VMEM] * (7 + len(halos)),
            out_specs=(VMEM,) * 4,
            scratch_shapes=scratch(rows, channels, width, hid, BIAS_ROWS),
            compiler_params=params,
            name="control",
        )(*halos, taps, gain, offset, w_in, w_out, land, filters)

    def conv_step(near, own, far):
        return pl.pallas_call(
            conv_kernel,
            out_shape=shape(rows, channels, width),
            in_specs=[VMEM] * 4,
            out_specs=VMEM,
            compiler_params=params,
            name="conv",
        )(near, own, far, taps)

    def tangent_step(ready, spare, inputs, unit, scale, slope, advanced):
        return pl.pallas_call(
            lambda *refs: tangent_kernel(ready, *refs),
            out_shape=shape(rows, channels + spare, width, kind=bf16),
            in_specs=[VMEM] * (9 + len(inputs)),
            out_specs=VMEM,
            scratch_shapes=scratch(rows, channels, width, hid, 0, not ready),
            compiler_params=params,
            name="tangent",
        )(*inputs, gain, w_in, w_out, land, filters, unit, scale, slope, advanced)

    near, far = exchange(member, range(1, members))
    control = member
    count = 2
    while count < members:
        sent = across(control, [(m, m + count) for m in range(0, count, 2) if m + count < members])
        control = jnp.where((me >= count) & (me < 2 * count), sent, control)
        count *= 2
    control, taps = lax.optimization_barrier((control, taps))
    control_other = across(control, partners)
    control_near, control_far = exchange(control, evens)
    conv = conv_step(near, member, far)
    control_near, control_far, conv, filters = lax.optimization_barrier((control_near, control_far, conv, filters))
    other = (across(control_far, partners), control_other, across(control_near, partners))
    control, unit, scale, slope = control_step(control_near, control, control_far, *other)
    for step in range(1, STEPS):
        halo = exchange(control, range(members))[0]
        inputs = (member, conv) if step == 1 else (near, member, far, taps)
        member = tangent_step(step == 1, SPARE, inputs, unit, scale, slope, control)
        halo, _ = lax.optimization_barrier((halo, member))
        other = across(halo, swapped)
        near, far = exchange(member, range(1, members))
        control, unit, scale, slope = control_step(halo, control, other)
    return tangent_step(False, 0, (near, member, far, taps), unit, scale, slope, control)[None]


def solution(mesh):
    in_specs = (
        P(("runs", "mem"), "lat", None, None),
        P("lat", None),
        P(),
        P(),
        P(),
        P(),
        P(),
        P(),
        P(),
    )
    out_specs = P(("runs", "mem"), "lat", None, None)
    return jax.shard_map(
        per_device, mesh=mesh, in_specs=in_specs, out_specs=out_specs, check_vma=False
    )
```

```python
import math

import jax
import jax.numpy as jnp
import numpy as np
from jax import lax
from jax.experimental import pallas as pl
from jax.experimental.pallas import tpu as pltpu
from jax.sharding import PartitionSpec as P

STEPS = 2
POLAR = 6
HALO = 3
TAPS = 7
GROUP = 16
LANES = 256
CHUNK = 64
BIAS_ROWS = 16
SPARE = 8

gelu_scale = 0.7978845608028654
gelu_cubic = 0.044715
epsilon = 1e-05

f32 = jnp.float32
bf16 = jnp.bfloat16


def fourier(width):
    index = np.arange(width, dtype=np.int32)
    wavenumber = np.where(index <= width // 2, index, index - width // 2).astype(np.int32)
    phase = index[:, None] * wavenumber[None, :] % width
    angle = phase.astype(np.float64) * (2.0 * math.pi / width)
    factor = np.where((index == 0) | (index == width // 2), 1.0 / math.sqrt(width), math.sqrt(2.0 / width))
    table = np.where(index[None, :] <= width // 2, np.cos(angle), np.sin(angle)) * factor[None, :]
    return table.astype(np.float32).astype(bf16)


def unroll(count, most):
    return max(u for u in range(1, most + 1) if count % u == 0)


def prepare_kernel(*refs):
    sources, refs = refs[:6], refs[6:]
    taps, gain_out, offset_out, w_in, land = refs[:5]
    kernel, gain, offset, weight_in, bias, land_mask, arrived = refs[5:]
    copies = [
        pltpu.make_async_copy(source, here, arrived.at[i])
        for i, (source, here) in enumerate(zip(sources, (kernel, gain, offset, weight_in, bias, land_mask)))
    ]
    for copy in copies:
        copy.start()
    for copy in copies:
        copy.wait()
    rows, _, channels, depth = taps.shape
    band = lax.axis_index("lat")
    lane = lax.broadcasted_iota(jnp.int32, (channels, depth), 1)
    here = lax.broadcasted_iota(jnp.int32, (channels, depth), 0)
    block = lane // GROUP
    turned = jnp.where(block < HALO, block + rows + HALO, jnp.where(block < HALO + rows, block, block - rows - HALO))
    block = jnp.where((band + lax.axis_index("mem")) % 2 == 1, block, turned)
    block = jnp.where(lane % GROUP == here % GROUP, block, -1)
    for j in range(TAPS):
        lines = [kernel[i, j : j + 1, :] for i in range(TAPS)] + [jnp.zeros((128 - TAPS, channels), f32)]
        turned = jnp.concatenate(lines, axis=0).T
        columns = [jnp.broadcast_to(turned[:, i : i + 1], (channels, depth)) for i in range(TAPS)]
        for r in range(rows):
            total = jnp.zeros((channels, depth), f32)
            for i in range(TAPS):
                total = jnp.where(block == r + i, columns[i], total)
            taps[r, j] = total.astype(bf16)
    gain_out[...] = jnp.broadcast_to(gain[...], (128, channels)).T
    offset_out[...] = jnp.broadcast_to(offset[...], (128, channels)).T
    w_in[:, :channels] = weight_in[...].astype(f32).T.astype(bf16)
    place = lax.broadcasted_iota(jnp.int32, (128, 128), 1)
    for k in range(bias.shape[0]):
        value = jnp.broadcast_to(bias[k : k + 1, :], (128, 128)).T
        high = value.astype(bf16).astype(f32)
        middle = (value - high).astype(bf16).astype(f32)
        low = value - high - middle
        three = jnp.where(place == 0, high, jnp.where(place == 1, middle, jnp.where(place == 2, low, 0.0)))
        w_in[k * 128 : (k + 1) * 128, channels:] = three[:, :BIAS_ROWS].astype(bf16)
    land[...] = land_mask[...].astype(f32)


def filter_kernel(bands, cutoff, table, out):
    rows, width, _ = out.shape
    band = lax.axis_index("lat")
    index = lax.broadcasted_iota(jnp.int32, (1, width), 1)
    wavenumber = jnp.where(index <= width // 2, index, index - width // 2)
    total_rows = rows * bands
    for r in range(rows):
        row = band * rows + r
        place = jnp.clip(jnp.where(row < POLAR, row, row - total_rows + 2 * POLAR), 0, 2 * POLAR - 1)
        kept = (table[...].astype(f32) * (wavenumber <= cutoff[place]).astype(f32)).astype(bf16)
        out[r] = lax.dot_general(
            kept, table[...], (((1,), (1,)), ((), ())), preferred_element_type=f32
        ).astype(bf16)
        if total_rows > 2 * POLAR:
            @pl.when((row >= POLAR) & (row < total_rows - POLAR))
            def _():
                across = lax.broadcasted_iota(jnp.int32, (width, width), 1)
                along = lax.broadcasted_iota(jnp.int32, (width, width), 0)
                out[r] = (across == along).astype(f32).astype(bf16)


def convolve(first, own, second, taps, out, most=10):
    rows, channels, width = out.shape

    def group(b, _):
        at = pl.ds(pl.multiple_of(b * GROUP, GROUP), GROUP)
        field = jnp.concatenate([first(at), own(at), second(at)], axis=0)
        field = field.reshape((rows + 2 * HALO) * GROUP, width)
        parts = jnp.dot(taps[:, :, at, :].reshape(rows * TAPS * GROUP, field.shape[0]), field, preferred_element_type=f32)
        for r in range(rows):
            part = [parts[(r * TAPS + j) * GROUP : (r * TAPS + j + 1) * GROUP] for j in range(TAPS)]
            total = part[HALO]
            for j in range(TAPS):
                if j != HALO:
                    total = total + pltpu.roll(part[j], (HALO - j) % width, 1)
            out[r, at, :] = total
        return 0

    groups = channels // GROUP
    lax.fori_loop(0, groups, group, 0, unroll=unroll(groups, most))


def read(ref):
    return lambda at: ref[:, at, :]


def choose(odd, first, other):
    return lambda at: jnp.where(odd, other[:, at, :], first[:, at, :])


def pipeline(rows, across, compact, first, second, third):
    def run(tiles):
        for i in range(len(tiles) + 2):
            for stage, lag in ((first, 0), (second, 1), (third, 2)):
                if lag <= i < len(tiles) + lag:
                    r, c = tiles[i - lag]
                    stage((i - lag) % 2, r, slice(c * LANES, (c + 1) * LANES))

    if compact:

        def one(r, _):
            run([(r, c) for c in range(across)])
            return 0

        lax.fori_loop(0, rows, one, 0)
    else:
        run([(r, c) for r in range(rows) for c in range(across)])


def row_of(r, channels):
    return pl.ds(pl.multiple_of(r * channels, GROUP), channels)


def add_bias_rows(normed, channels):
    row = lax.broadcasted_iota(jnp.int32, (BIAS_ROWS, normed.shape[1]), 0)
    normed[channels:, :] = jnp.where(row < 3, 1.0, 0.0).astype(bf16)


def polar_filter(raw, filters, out, r):
    channels = raw.shape[0] // filters.shape[0]
    out[r, :channels, :] = jnp.dot(
        raw[row_of(r, channels), :], filters[r], preferred_element_type=f32
    ).astype(bf16)


def control_kernel(*refs):
    first_halo, own, second_halo = refs[:3]
    refs = refs[3:]
    other = None
    if len(refs) > 19:
        other, refs = refs[:3], refs[3:]
    (
        taps, gain, bias, w_in, w_out, land, filters,
        out, unit_out, scale_out, slope_out, conv, normed, normed_b, hidden, hidden_b, act, act_b, raw,
    ) = refs
    rows, channels, width = out.shape
    hid = w_in.shape[0]
    normed, hidden, act = (normed, normed_b), (hidden, hidden_b), (act, act_b)
    odd = lax.axis_index("mem") % 2 == 1
    for block in normed:
        add_bias_rows(block, channels)
    blocks = [read(first_halo), read(own), read(second_halo)]
    if other is not None:
        blocks = [choose(odd, a, b) for a, b in zip((first_halo, own, second_halo), other)]
    convolve(*blocks, taps, conv, 10 if other is not None else 2)
    across = width // LANES

    def first(slot, r, at):
        for w in range(0, LANES, 128):
            here, there = slice(at.start + w, at.start + w + 128), slice(w, w + 128)
            value = conv[r, :, here]
            centered = value - jnp.mean(value, axis=0, keepdims=True)
            scale = lax.rsqrt(jnp.mean(centered * centered, axis=0, keepdims=True) + epsilon)
            unit = centered * scale
            unit_out[r, :, here] = unit
            scale_out[r, :, here] = scale
            normed[slot][:channels, there] = (unit * gain[...] + bias[...]).astype(bf16)
        hidden[slot][...] = jnp.dot(w_in[...], normed[slot][...], preferred_element_type=f32)

    def pair(slot, r, at):
        for c in range(0, hid, CHUNK):
            h = hidden[slot][c : c + CHUNK, :]
            square = h * h
            t = jnp.tanh(h * (gelu_scale + (gelu_scale * gelu_cubic) * square))
            half = 0.5 + 0.5 * t
            act[slot][c : c + CHUNK, :] = (h * half).astype(bf16)
            lean = h * (2.0 * gelu_scale + (6.0 * gelu_scale * gelu_cubic) * square)
            slope_out[r, c : c + CHUNK, at] = half * (1.0 + (1.0 - half) * lean)

    def third(slot, r, at):
        update = jnp.dot(w_out[...], act[slot][...], preferred_element_type=f32)
        field = own[r, :, at]
        if other is not None:
            field = jnp.where(odd, other[1][r, :, at], field)
        raw[row_of(r, channels), at] = (land[pl.ds(r, 1), at] * (field.astype(f32) + update)).astype(bf16)
        if at.stop == width:
            polar_filter(raw, filters, out, r)

    pipeline(rows, across, other is None, first, pair, third)


def conv_kernel(first, own, second, taps, out):
    convolve(read(first), read(own), read(second), taps, out, 5)


def tangent_kernel(ready, *refs):
    if ready:
        own, conv = refs[:2]
        refs = refs[2:]
    else:
        near, own, far, taps = refs[:4]
        refs = refs[4:]
    gain, w_in, w_out, land, filters, unit_in, scale_in, slope_in, advanced, out = refs[:10]
    refs = refs[10:]
    if not ready:
        conv, refs = refs[0], refs[1:]
    normed, normed_b, hidden, hidden_b, act, act_b, raw = refs
    normed, hidden, act = (normed, normed_b), (hidden, hidden_b), (act, act_b)
    rows, channels, width = advanced.shape
    hid = w_in.shape[0]
    across = width // LANES
    is_control = lax.axis_index("mem") == 0

    def first(slot, r, at):
        for w in range(0, LANES, 128):
            here, there = slice(at.start + w, at.start + w + 128), slice(w, w + 128)
            value = conv[r, :, here]
            unit = unit_in[r, :, here]
            average = jnp.mean(value, axis=0, keepdims=True)
            along = jnp.mean(value * unit, axis=0, keepdims=True)
            normed[slot][:, there] = (gain[...] * scale_in[r, :, here] * (value - average - unit * along)).astype(bf16)
        hidden[slot][...] = jnp.dot(w_in[:, :channels], normed[slot][...], preferred_element_type=f32)

    def mix(slot, r, at):
        for c in range(0, hid, CHUNK):
            act[slot][c : c + CHUNK, :] = (slope_in[r, c : c + CHUNK, at] * hidden[slot][c : c + CHUNK, :]).astype(bf16)

    def third(slot, r, at):
        update = jnp.dot(w_out[...], act[slot][...], preferred_element_type=f32)
        raw[row_of(r, channels), at] = (
            land[pl.ds(r, 1), at] * (own[r, :channels, at].astype(f32) + update)
        ).astype(bf16)
        if at.stop == width:
            polar_filter(raw, filters, out, r)

    if out.shape[1] > channels:
        out[:, channels:, :] = jnp.zeros((rows, out.shape[1] - channels, width), bf16)

    @pl.when(is_control)
    def _():
        out[:, :channels, :] = advanced[...]

    @pl.when(jnp.logical_not(is_control))
    def _():
        if not ready:
            convolve(read(near), read(own), read(far), taps, conv)
        pipeline(rows, across, False, first, mix, third)


def scratch(rows, channels, width, hid, bias_rows, conv=True):
    return ([pltpu.VMEM((rows, channels, width), f32)] if conv else []) + [
        pltpu.VMEM((channels + bias_rows, LANES), bf16),
        pltpu.VMEM((channels + bias_rows, LANES), bf16),
        pltpu.VMEM((hid, LANES), f32),
        pltpu.VMEM((hid, LANES), f32),
        pltpu.VMEM((hid, LANES), bf16),
        pltpu.VMEM((hid, LANES), bf16),
        pltpu.VMEM((rows * channels, width), bf16),
    ]


SMEM = pl.BlockSpec(memory_space=pltpu.SMEM)
VMEM = pl.BlockSpec(memory_space=pltpu.VMEM)
LIMIT = 24 << 20


def per_device(
    states, land_mask, cutoff, kernel, norm_gain, norm_bias, weight_in, bias_in, weight_out
):
    member = states[0]
    rows, channels, width = member.shape
    hid = weight_in.shape[1]
    bands = lax.axis_size("lat")
    members = lax.axis_size("mem")
    me = lax.axis_index("mem")
    params = pltpu.CompilerParams(vmem_limit_bytes=LIMIT)

    def shape(*dims, kind=f32):
        return jax.ShapeDtypeStruct(dims, kind)

    field = shape(rows, channels, width, kind=bf16)

    def send(block, pairs):
        return lax.ppermute(block, ("mem", "lat"), [(a * bands + i, b * bands + j) for (a, i), (b, j) in pairs])

    def neighbours(which, start):
        pairs = [((m, z), (m, z + 1)) for m in which for z in range(start, bands - 1, 2)]
        return pairs + [(b, a) for a, b in pairs]

    def exchange(block, which):
        even, odd = [m for m in which if m % 2 == 0], [m for m in which if m % 2 == 1]
        first = send(block, neighbours(even, 0) + neighbours(odd, 1))
        return first, send(block, neighbours(even, 1) + neighbours(odd, 0))

    def across(block, pairs):
        return send(block, [((a, z), (b, z)) for a, b in pairs for z in range(bands)])

    evens = list(range(0, members, 2))
    odds = list(range(1, members, 2))
    partners = [(m - 1, m) for m in odds]
    swapped = partners + [(b, a) for a, b in partners]

    table = jnp.asarray(fourier(width))
    w_out = weight_out.T
    sources = (kernel, norm_gain[None], norm_bias[None], weight_in, bias_in.reshape(-1, 128), land_mask)
    taps, gain, offset, w_in, land = pl.pallas_call(
        prepare_kernel,
        out_shape=(
            shape(rows, TAPS, channels, (rows + 2 * HALO) * GROUP, kind=bf16),
            shape(channels, 128),
            shape(channels, 128),
            shape(hid, channels + BIAS_ROWS, kind=bf16),
            shape(rows, width),
        ),
        in_specs=[pl.BlockSpec(memory_space=pltpu.MemorySpace.HBM)] * 6,
        out_specs=(VMEM,) * 5,
        scratch_shapes=[pltpu.VMEM(x.shape, x.dtype) for x in sources] + [pltpu.SemaphoreType.DMA((6,))],
        compiler_params=params,
        name="prepare",
    )(*sources)
    filters = pl.pallas_call(
        lambda *refs: filter_kernel(bands, *refs),
        out_shape=shape(rows, width, width, kind=bf16),
        in_specs=[SMEM, VMEM],
        out_specs=VMEM,
        compiler_params=params,
        name="filters",
    )(cutoff, table)

    def control_step(*halos):
        return pl.pallas_call(
            control_kernel,
            out_shape=(field, shape(rows, channels, width), shape(rows, 1, width), shape(rows, hid, width)),
            in_specs=[VMEM] * (7 + len(halos)),
            out_specs=(VMEM,) * 4,
            scratch_shapes=scratch(rows, channels, width, hid, BIAS_ROWS),
            compiler_params=params,
            name="control",
        )(*halos, taps, gain, offset, w_in, w_out, land, filters)

    def conv_step(near, own, far):
        return pl.pallas_call(
            conv_kernel,
            out_shape=shape(rows, channels, width),
            in_specs=[VMEM] * 4,
            out_specs=VMEM,
            compiler_params=params,
            name="conv",
        )(near, own, far, taps)

    def tangent_step(ready, spare, inputs, unit, scale, slope, advanced):
        return pl.pallas_call(
            lambda *refs: tangent_kernel(ready, *refs),
            out_shape=shape(rows, channels + spare, width, kind=bf16),
            in_specs=[VMEM] * (9 + len(inputs)),
            out_specs=VMEM,
            scratch_shapes=scratch(rows, channels, width, hid, 0, not ready),
            compiler_params=params,
            name="tangent",
        )(*inputs, gain, w_in, w_out, land, filters, unit, scale, slope, advanced)

    near, far = exchange(member, range(1, members))
    control = member
    count = 2
    while count < members:
        sent = across(control, [(m, m + count) for m in range(0, count, 2) if m + count < members])
        control = jnp.where((me >= count) & (me < 2 * count), sent, control)
        count *= 2
    control, taps = lax.optimization_barrier((control, taps))
    control_other = across(control, partners)
    control_near, control_far = exchange(control, evens)
    conv = conv_step(near, member, far)
    control_near, control_far, conv, filters = lax.optimization_barrier((control_near, control_far, conv, filters))
    other = (across(control_far, partners), control_other, across(control_near, partners))
    control, unit, scale, slope = control_step(control_near, control, control_far, *other)
    for step in range(1, STEPS):
        halo = exchange(control, range(members))[0]
        inputs = (member, conv) if step == 1 else (near, member, far, taps)
        member = tangent_step(step == 1, SPARE, inputs, unit, scale, slope, control)
        halo, _ = lax.optimization_barrier((halo, member))
        other = across(halo, swapped)
        near, far = exchange(member, range(1, members))
        control, unit, scale, slope = control_step(halo, control, other)
    return tangent_step(False, 0, (near, member, far, taps), unit, scale, slope, control)[None]


def solution(mesh):
    in_specs = (
        P(("runs", "mem"), "lat", None, None),
        P("lat", None),
        P(),
        P(),
        P(),
        P(),
        P(),
        P(),
        P(),
    )
    out_specs = P(("runs", "mem"), "lat", None, None)
    return jax.shard_map(
        per_device, mesh=mesh, in_specs=in_specs, out_specs=out_specs, check_vma=False
    )
```

```python
import math

import jax
import jax.numpy as jnp
import numpy as np
from jax import lax
from jax.experimental import pallas as pl
from jax.experimental.pallas import tpu as pltpu
from jax.sharding import PartitionSpec as P

STEPS = 2
POLAR = 6
HALO = 3
TAPS = 7
GROUP = 16
LANES = 256
CHUNK = 64
BIAS_ROWS = 16
SPARE = 8

gelu_scale = 0.7978845608028654
gelu_cubic = 0.044715
epsilon = 1e-05

f32 = jnp.float32
bf16 = jnp.bfloat16


def fourier(width):
    index = np.arange(width, dtype=np.int32)
    wavenumber = np.where(index <= width // 2, index, index - width // 2).astype(np.int32)
    phase = index[:, None] * wavenumber[None, :] % width
    angle = phase.astype(np.float64) * (2.0 * math.pi / width)
    factor = np.where((index == 0) | (index == width // 2), 1.0 / math.sqrt(width), math.sqrt(2.0 / width))
    table = np.where(index[None, :] <= width // 2, np.cos(angle), np.sin(angle)) * factor[None, :]
    return table.astype(np.float32).astype(bf16)


def unroll(count, most):
    return max(u for u in range(1, most + 1) if count % u == 0)


def prepare_kernel(*refs):
    sources, refs = refs[:6], refs[6:]
    taps, gain_out, offset_out, w_in, land = refs[:5]
    kernel, gain, offset, weight_in, bias, land_mask, arrived = refs[5:]
    copies = [
        pltpu.make_async_copy(source, here, arrived.at[i])
        for i, (source, here) in enumerate(zip(sources, (kernel, gain, offset, weight_in, bias, land_mask)))
    ]
    for copy in copies:
        copy.start()
    for copy in copies:
        copy.wait()
    rows, _, channels, depth = taps.shape
    band = lax.axis_index("lat")
    lane = lax.broadcasted_iota(jnp.int32, (channels, depth), 1)
    here = lax.broadcasted_iota(jnp.int32, (channels, depth), 0)
    block = lane // GROUP
    turned = jnp.where(block < HALO, block + rows + HALO, jnp.where(block < HALO + rows, block, block - rows - HALO))
    block = jnp.where((band + lax.axis_index("mem")) % 2 == 1, block, turned)
    block = jnp.where(lane % GROUP == here % GROUP, block, -1)
    for j in range(TAPS):
        lines = [kernel[i, j : j + 1, :] for i in range(TAPS)] + [jnp.zeros((128 - TAPS, channels), f32)]
        turned = jnp.concatenate(lines, axis=0).T
        columns = [jnp.broadcast_to(turned[:, i : i + 1], (channels, depth)) for i in range(TAPS)]
        for r in range(rows):
            total = jnp.zeros((channels, depth), f32)
            for i in range(TAPS):
                total = jnp.where(block == r + i, columns[i], total)
            taps[r, j] = total.astype(bf16)
    gain_out[...] = jnp.broadcast_to(gain[...], (128, channels)).T
    offset_out[...] = jnp.broadcast_to(offset[...], (128, channels)).T
    w_in[:, :channels] = weight_in[...].astype(f32).T.astype(bf16)
    place = lax.broadcasted_iota(jnp.int32, (128, 128), 1)
    for k in range(bias.shape[0]):
        value = jnp.broadcast_to(bias[k : k + 1, :], (128, 128)).T
        high = value.astype(bf16).astype(f32)
        middle = (value - high).astype(bf16).astype(f32)
        low = value - high - middle
        three = jnp.where(place == 0, high, jnp.where(place == 1, middle, jnp.where(place == 2, low, 0.0)))
        w_in[k * 128 : (k + 1) * 128, channels:] = three[:, :BIAS_ROWS].astype(bf16)
    land[...] = land_mask[...].astype(f32)


def filter_kernel(bands, cutoff, table, out):
    rows, width, _ = out.shape
    band = lax.axis_index("lat")
    index = lax.broadcasted_iota(jnp.int32, (1, width), 1)
    wavenumber = jnp.where(index <= width // 2, index, index - width // 2)
    total_rows = rows * bands
    for r in range(rows):
        row = band * rows + r
        place = jnp.clip(jnp.where(row < POLAR, row, row - total_rows + 2 * POLAR), 0, 2 * POLAR - 1)
        kept = (table[...].astype(f32) * (wavenumber <= cutoff[place]).astype(f32)).astype(bf16)
        out[r] = lax.dot_general(
            kept, table[...], (((1,), (1,)), ((), ())), preferred_element_type=f32
        ).astype(bf16)
        if total_rows > 2 * POLAR:
            @pl.when((row >= POLAR) & (row < total_rows - POLAR))
            def _():
                across = lax.broadcasted_iota(jnp.int32, (width, width), 1)
                along = lax.broadcasted_iota(jnp.int32, (width, width), 0)
                out[r] = (across == along).astype(f32).astype(bf16)


def convolve(first, own, second, taps, out, most=10):
    rows, channels, width = out.shape

    def group(b, _):
        at = pl.ds(pl.multiple_of(b * GROUP, GROUP), GROUP)
        field = jnp.concatenate([first(at), own(at), second(at)], axis=0)
        field = field.reshape((rows + 2 * HALO) * GROUP, width)
        parts = jnp.dot(taps[:, :, at, :].reshape(rows * TAPS * GROUP, field.shape[0]), field, preferred_element_type=f32)
        for r in range(rows):
            part = [parts[(r * TAPS + j) * GROUP : (r * TAPS + j + 1) * GROUP] for j in range(TAPS)]
            total = part[HALO]
            for j in range(TAPS):
                if j != HALO:
                    total = total + pltpu.roll(part[j], (HALO - j) % width, 1)
            out[r, at, :] = total
        return 0

    groups = channels // GROUP
    lax.fori_loop(0, groups, group, 0, unroll=unroll(groups, most))


def read(ref):
    return lambda at: ref[:, at, :]


def choose(odd, first, other):
    return lambda at: jnp.where(odd, other[:, at, :], first[:, at, :])


def pipeline(rows, across, compact, first, second, third):
    def run(tiles):
        for i in range(len(tiles) + 2):
            for stage, lag in ((first, 0), (second, 1), (third, 2)):
                if lag <= i < len(tiles) + lag:
                    r, c = tiles[i - lag]
                    stage((i - lag) % 2, r, slice(c * LANES, (c + 1) * LANES))

    if compact:

        def one(r, _):
            run([(r, c) for c in range(across)])
            return 0

        lax.fori_loop(0, rows, one, 0)
    else:
        run([(r, c) for r in range(rows) for c in range(across)])


def row_of(r, channels):
    return pl.ds(pl.multiple_of(r * channels, GROUP), channels)


def add_bias_rows(normed, channels):
    row = lax.broadcasted_iota(jnp.int32, (BIAS_ROWS, normed.shape[1]), 0)
    normed[channels:, :] = jnp.where(row < 3, 1.0, 0.0).astype(bf16)


def polar_filter(raw, filters, out, r):
    channels = raw.shape[0] // filters.shape[0]
    out[r, :channels, :] = jnp.dot(
        raw[row_of(r, channels), :], filters[r], preferred_element_type=f32
    ).astype(bf16)


def gelu_parts(h, both=True):
    square = h * h
    half = 0.5 + 0.5 * jnp.tanh(h * (gelu_scale + (gelu_scale * gelu_cubic) * square))
    return half, h * (2.0 * gelu_scale + (6.0 * gelu_scale * gelu_cubic) * square) if both else None


def gelu_slope(half, lean):
    return half * (1.0 + (1.0 - half) * lean)


def control_kernel(*refs):
    first_halo, own, second_halo = refs[:3]
    refs = refs[3:]
    other = None
    if len(refs) > 19:
        other, refs = refs[:3], refs[3:]
    (
        taps, gain, bias, w_in, w_out, land, filters,
        out, unit_out, scale_out, slope_out, conv, normed, normed_b, hidden, hidden_b, act, act_b, raw,
    ) = refs
    rows, channels, width = out.shape
    hid = w_in.shape[0]
    normed, hidden, act = (normed, normed_b), (hidden, hidden_b), (act, act_b)
    odd = lax.axis_index("mem") % 2 == 1
    for block in normed:
        add_bias_rows(block, channels)
    blocks = [read(first_halo), read(own), read(second_halo)]
    if other is not None:
        blocks = [choose(odd, a, b) for a, b in zip((first_halo, own, second_halo), other)]
    convolve(*blocks, taps, conv, 10 if other is not None else 2)
    across = width // LANES

    def first(slot, r, at):
        for w in range(0, LANES, 128):
            here, there = slice(at.start + w, at.start + w + 128), slice(w, w + 128)
            value = conv[r, :, here]
            centered = value - jnp.mean(value, axis=0, keepdims=True)
            scale = lax.rsqrt(jnp.mean(centered * centered, axis=0, keepdims=True) + epsilon)
            unit = centered * scale
            unit_out[r, :, here] = unit
            scale_out[r, :, here] = scale
            normed[slot][:channels, there] = (unit * gain[...] + bias[...]).astype(bf16)
        hidden[slot][...] = jnp.dot(w_in[...], normed[slot][...], preferred_element_type=f32)

    def pair(slot, r, at):
        for c in range(0, hid, CHUNK):
            h = hidden[slot][c : c + CHUNK, :]
            half, lean = gelu_parts(h, other is None)
            act[slot][c : c + CHUNK, :] = (h * half).astype(bf16)
            if other is None:
                slope_out[r, c : c + CHUNK, at] = gelu_slope(half, lean)
            else:
                slope_out[r, c : c + CHUNK, at] = h

    def third(slot, r, at):
        update = jnp.dot(w_out[...], act[slot][...], preferred_element_type=f32)
        field = own[r, :, at]
        if other is not None:
            field = jnp.where(odd, other[1][r, :, at], field)
        raw[row_of(r, channels), at] = (land[pl.ds(r, 1), at] * (field.astype(f32) + update)).astype(bf16)
        if at.stop == width:
            polar_filter(raw, filters, out, r)

    pipeline(rows, across, other is None, first, pair, third)


def conv_kernel(first, own, second, taps, out):
    convolve(read(first), read(own), read(second), taps, out, 5)


def tangent_kernel(ready, *refs):
    if ready:
        own, conv = refs[:2]
        refs = refs[2:]
    else:
        near, own, far, taps = refs[:4]
        refs = refs[4:]
    gain, w_in, w_out, land, filters, unit_in, scale_in, slope_in, advanced, out = refs[:10]
    refs = refs[10:]
    if not ready:
        conv, refs = refs[0], refs[1:]
    normed, normed_b, hidden, hidden_b, act, act_b, raw = refs
    normed, hidden, act = (normed, normed_b), (hidden, hidden_b), (act, act_b)
    rows, channels, width = advanced.shape
    hid = w_in.shape[0]
    across = width // LANES
    is_control = lax.axis_index("mem") == 0

    def first(slot, r, at):
        for w in range(0, LANES, 128):
            here, there = slice(at.start + w, at.start + w + 128), slice(w, w + 128)
            value = conv[r, :, here]
            unit = unit_in[r, :, here]
            average = jnp.mean(value, axis=0, keepdims=True)
            along = jnp.mean(value * unit, axis=0, keepdims=True)
            normed[slot][:, there] = (gain[...] * scale_in[r, :, here] * (value - average - unit * along)).astype(bf16)
        hidden[slot][...] = jnp.dot(w_in[:, :channels], normed[slot][...], preferred_element_type=f32)

    def mix(slot, r, at):
        for c in range(0, hid, CHUNK):
            slope = slope_in[r, c : c + CHUNK, at]
            if ready:
                slope = gelu_slope(*gelu_parts(slope))
            act[slot][c : c + CHUNK, :] = (slope * hidden[slot][c : c + CHUNK, :]).astype(bf16)

    def third(slot, r, at):
        update = jnp.dot(w_out[...], act[slot][...], preferred_element_type=f32)
        raw[row_of(r, channels), at] = (
            land[pl.ds(r, 1), at] * (own[r, :channels, at].astype(f32) + update)
        ).astype(bf16)
        if at.stop == width:
            polar_filter(raw, filters, out, r)

    if out.shape[1] > channels:
        out[:, channels:, :] = jnp.zeros((rows, out.shape[1] - channels, width), bf16)

    @pl.when(is_control)
    def _():
        out[:, :channels, :] = advanced[...]

    @pl.when(jnp.logical_not(is_control))
    def _():
        if not ready:
            convolve(read(near), read(own), read(far), taps, conv)
        pipeline(rows, across, False, first, mix, third)


def scratch(rows, channels, width, hid, bias_rows, conv=True):
    return ([pltpu.VMEM((rows, channels, width), f32)] if conv else []) + [
        pltpu.VMEM((channels + bias_rows, LANES), bf16),
        pltpu.VMEM((channels + bias_rows, LANES), bf16),
        pltpu.VMEM((hid, LANES), f32),
        pltpu.VMEM((hid, LANES), f32),
        pltpu.VMEM((hid, LANES), bf16),
        pltpu.VMEM((hid, LANES), bf16),
        pltpu.VMEM((rows * channels, width), bf16),
    ]


SMEM = pl.BlockSpec(memory_space=pltpu.SMEM)
VMEM = pl.BlockSpec(memory_space=pltpu.VMEM)
LIMIT = 24 << 20


def per_device(
    states, land_mask, cutoff, kernel, norm_gain, norm_bias, weight_in, bias_in, weight_out
):
    member = states[0]
    rows, channels, width = member.shape
    hid = weight_in.shape[1]
    bands = lax.axis_size("lat")
    members = lax.axis_size("mem")
    me = lax.axis_index("mem")
    params = pltpu.CompilerParams(vmem_limit_bytes=LIMIT)

    def shape(*dims, kind=f32):
        return jax.ShapeDtypeStruct(dims, kind)

    field = shape(rows, channels, width, kind=bf16)

    def send(block, pairs):
        return lax.ppermute(block, ("mem", "lat"), [(a * bands + i, b * bands + j) for (a, i), (b, j) in pairs])

    def neighbours(which, start):
        pairs = [((m, z), (m, z + 1)) for m in which for z in range(start, bands - 1, 2)]
        return pairs + [(b, a) for a, b in pairs]

    def exchange(block, which):
        even, odd = [m for m in which if m % 2 == 0], [m for m in which if m % 2 == 1]
        first = send(block, neighbours(even, 0) + neighbours(odd, 1))
        return first, send(block, neighbours(even, 1) + neighbours(odd, 0))

    def across(block, pairs):
        return send(block, [((a, z), (b, z)) for a, b in pairs for z in range(bands)])

    evens = list(range(0, members, 2))
    odds = list(range(1, members, 2))
    partners = [(m - 1, m) for m in odds]
    swapped = partners + [(b, a) for a, b in partners]

    table = jnp.asarray(fourier(width))
    w_out = weight_out.T
    sources = (kernel, norm_gain[None], norm_bias[None], weight_in, bias_in.reshape(-1, 128), land_mask)
    taps, gain, offset, w_in, land = pl.pallas_call(
        prepare_kernel,
        out_shape=(
            shape(rows, TAPS, channels, (rows + 2 * HALO) * GROUP, kind=bf16),
            shape(channels, 128),
            shape(channels, 128),
            shape(hid, channels + BIAS_ROWS, kind=bf16),
            shape(rows, width),
        ),
        in_specs=[pl.BlockSpec(memory_space=pltpu.MemorySpace.HBM)] * 6,
        out_specs=(VMEM,) * 5,
        scratch_shapes=[pltpu.VMEM(x.shape, x.dtype) for x in sources] + [pltpu.SemaphoreType.DMA((6,))],
        compiler_params=params,
        name="prepare",
    )(*sources)
    filters = pl.pallas_call(
        lambda *refs: filter_kernel(bands, *refs),
        out_shape=shape(rows, width, width, kind=bf16),
        in_specs=[SMEM, VMEM],
        out_specs=VMEM,
        compiler_params=params,
        name="filters",
    )(cutoff, table)

    def control_step(*halos):
        return pl.pallas_call(
            control_kernel,
            out_shape=(field, shape(rows, channels, width), shape(rows, 1, width), shape(rows, hid, width)),
            in_specs=[VMEM] * (7 + len(halos)),
            out_specs=(VMEM,) * 4,
            scratch_shapes=scratch(rows, channels, width, hid, BIAS_ROWS),
            compiler_params=params,
            name="control",
        )(*halos, taps, gain, offset, w_in, w_out, land, filters)

    def conv_step(near, own, far):
        return pl.pallas_call(
            conv_kernel,
            out_shape=shape(rows, channels, width),
            in_specs=[VMEM] * 4,
            out_specs=VMEM,
            compiler_params=params,
            name="conv",
        )(near, own, far, taps)

    def tangent_step(ready, spare, inputs, unit, scale, slope, advanced):
        return pl.pallas_call(
            lambda *refs: tangent_kernel(ready, *refs),
            out_shape=shape(rows, channels + spare, width, kind=bf16),
            in_specs=[VMEM] * (9 + len(inputs)),
            out_specs=VMEM,
            scratch_shapes=scratch(rows, channels, width, hid, 0, not ready),
            compiler_params=params,
            name="tangent",
        )(*inputs, gain, w_in, w_out, land, filters, unit, scale, slope, advanced)

    near, far = exchange(member, range(1, members))
    control = member
    count = 2
    while count < members:
        sent = across(control, [(m, m + count) for m in range(0, count, 2) if m + count < members])
        control = jnp.where((me >= count) & (me < 2 * count), sent, control)
        count *= 2
    control, taps = lax.optimization_barrier((control, taps))
    control_other = across(control, partners)
    control_near, control_far = exchange(control, evens)
    conv = conv_step(near, member, far)
    control_near, control_far, conv, filters = lax.optimization_barrier((control_near, control_far, conv, filters))
    other = (across(control_far, partners), control_other, across(control_near, partners))
    control, unit, scale, slope = control_step(control_near, control, control_far, *other)
    for step in range(1, STEPS):
        halo = exchange(control, range(members))[0]
        inputs = (member, conv) if step == 1 else (near, member, far, taps)
        member = tangent_step(step == 1, SPARE, inputs, unit, scale, slope, control)
        halo, _ = lax.optimization_barrier((halo, member))
        other = across(halo, swapped)
        near, far = exchange(member, range(1, members))
        control, unit, scale, slope = control_step(halo, control, other)
    return tangent_step(False, 0, (near, member, far, taps), unit, scale, slope, control)[None]


def solution(mesh):
    in_specs = (
        P(("runs", "mem"), "lat", None, None),
        P("lat", None),
        P(),
        P(),
        P(),
        P(),
        P(),
        P(),
        P(),
    )
    out_specs = P(("runs", "mem"), "lat", None, None)
    return jax.shard_map(
        per_device, mesh=mesh, in_specs=in_specs, out_specs=out_specs, check_vma=False
    )
```

```python
import math

import jax
import jax.numpy as jnp
import numpy as np
from jax import lax
from jax.experimental import pallas as pl
from jax.experimental.pallas import tpu as pltpu
from jax.sharding import PartitionSpec as P

STEPS = 2
POLAR = 6
HALO = 3
TAPS = 7
GROUP = 16
LANES = 256
CHUNK = 64
BIAS_ROWS = 16

gelu_scale = 0.7978845608028654
gelu_cubic = 0.044715
epsilon = 1e-05

f32 = jnp.float32
bf16 = jnp.bfloat16


def fourier(width):
    index = np.arange(width, dtype=np.int32)
    wavenumber = np.where(index <= width // 2, index, index - width // 2).astype(np.int32)
    phase = index[:, None] * wavenumber[None, :] % width
    angle = phase.astype(np.float64) * (2.0 * math.pi / width)
    factor = np.where((index == 0) | (index == width // 2), 1.0 / math.sqrt(width), math.sqrt(2.0 / width))
    table = np.where(index[None, :] <= width // 2, np.cos(angle), np.sin(angle)) * factor[None, :]
    return table.astype(np.float32).astype(bf16)


def unroll(count, most):
    return max(u for u in range(1, most + 1) if count % u == 0)


def prepare_kernel(*refs):
    sources, refs = refs[:6], refs[6:]
    taps, gain_out, offset_out, w_in, land = refs[:5]
    kernel, gain, offset, weight_in, bias, land_mask, arrived = refs[5:]
    copies = [
        pltpu.make_async_copy(source, here, arrived.at[i])
        for i, (source, here) in enumerate(zip(sources, (kernel, gain, offset, weight_in, bias, land_mask)))
    ]
    for copy in copies:
        copy.start()
    for copy in copies:
        copy.wait()
    rows, _, channels, depth = taps.shape
    band = lax.axis_index("lat")
    lane = lax.broadcasted_iota(jnp.int32, (channels, depth), 1)
    here = lax.broadcasted_iota(jnp.int32, (channels, depth), 0)
    block = lane // GROUP
    turned = jnp.where(block < HALO, block + rows + HALO, jnp.where(block < HALO + rows, block, block - rows - HALO))
    block = jnp.where((band + lax.axis_index("mem")) % 2 == 1, block, turned)
    block = jnp.where(lane % GROUP == here % GROUP, block, -1)
    for j in range(TAPS):
        lines = [kernel[i, j : j + 1, :] for i in range(TAPS)] + [jnp.zeros((128 - TAPS, channels), f32)]
        turned = jnp.concatenate(lines, axis=0).T
        columns = [jnp.broadcast_to(turned[:, i : i + 1], (channels, depth)) for i in range(TAPS)]
        for r in range(rows):
            total = jnp.zeros((channels, depth), f32)
            for i in range(TAPS):
                total = jnp.where(block == r + i, columns[i], total)
            taps[r, j] = total.astype(bf16)
    gain_out[...] = jnp.broadcast_to(gain[...], (128, channels)).T
    offset_out[...] = jnp.broadcast_to(offset[...], (128, channels)).T
    w_in[:, :channels] = weight_in[...].astype(f32).T.astype(bf16)
    place = lax.broadcasted_iota(jnp.int32, (128, 128), 1)
    for k in range(bias.shape[0]):
        value = jnp.broadcast_to(bias[k : k + 1, :], (128, 128)).T
        high = value.astype(bf16).astype(f32)
        middle = (value - high).astype(bf16).astype(f32)
        low = value - high - middle
        three = jnp.where(place == 0, high, jnp.where(place == 1, middle, jnp.where(place == 2, low, 0.0)))
        w_in[k * 128 : (k + 1) * 128, channels:] = three[:, :BIAS_ROWS].astype(bf16)
    land[...] = land_mask[...].astype(f32)


def filter_kernel(bands, cutoff, table, out):
    rows, width, _ = out.shape
    band = lax.axis_index("lat")
    index = lax.broadcasted_iota(jnp.int32, (1, width), 1)
    wavenumber = jnp.where(index <= width // 2, index, index - width // 2)
    total_rows = rows * bands
    for r in range(rows):
        row = band * rows + r
        place = jnp.clip(jnp.where(row < POLAR, row, row - total_rows + 2 * POLAR), 0, 2 * POLAR - 1)
        kept = (table[...].astype(f32) * (wavenumber <= cutoff[place]).astype(f32)).astype(bf16)
        out[r] = lax.dot_general(
            kept, table[...], (((1,), (1,)), ((), ())), preferred_element_type=f32
        ).astype(bf16)
        if total_rows > 2 * POLAR:
            @pl.when((row >= POLAR) & (row < total_rows - POLAR))
            def _():
                across = lax.broadcasted_iota(jnp.int32, (width, width), 1)
                along = lax.broadcasted_iota(jnp.int32, (width, width), 0)
                out[r] = (across == along).astype(f32).astype(bf16)


def convolve(first, own, second, taps, out, most=10):
    rows, channels, width = out.shape

    def group(b, _):
        at = pl.ds(pl.multiple_of(b * GROUP, GROUP), GROUP)
        field = jnp.concatenate([first(at), own(at), second(at)], axis=0)
        field = field.reshape((rows + 2 * HALO) * GROUP, width)
        parts = jnp.dot(taps[:, :, at, :].reshape(rows * TAPS * GROUP, field.shape[0]), field, preferred_element_type=f32)
        for r in range(rows):
            part = [parts[(r * TAPS + j) * GROUP : (r * TAPS + j + 1) * GROUP] for j in range(TAPS)]
            total = part[HALO]
            for j in range(TAPS):
                if j != HALO:
                    total = total + pltpu.roll(part[j], (HALO - j) % width, 1)
            out[r, at, :] = total
        return 0

    groups = channels // GROUP
    lax.fori_loop(0, groups, group, 0, unroll=unroll(groups, most))


def read(ref):
    return lambda at: ref[:, at, :]


def choose(odd, first, other):
    return lambda at: jnp.where(odd, other[:, at, :], first[:, at, :])


def pipeline(rows, across, compact, first, second, third):
    def run(tiles):
        for i in range(len(tiles) + 2):
            for stage, lag in ((first, 0), (second, 1), (third, 2)):
                if lag <= i < len(tiles) + lag:
                    r, c = tiles[i - lag]
                    stage((i - lag) % 2, r, slice(c * LANES, (c + 1) * LANES))

    if compact:

        def one(r, _):
            run([(r, c) for c in range(across)])
            return 0

        lax.fori_loop(0, rows, one, 0)
    else:
        run([(r, c) for r in range(rows) for c in range(across)])


def row_of(r, channels):
    return pl.ds(pl.multiple_of(r * channels, GROUP), channels)


def add_bias_rows(normed, channels):
    row = lax.broadcasted_iota(jnp.int32, (BIAS_ROWS, normed.shape[1]), 0)
    normed[channels:, :] = jnp.where(row < 3, 1.0, 0.0).astype(bf16)


def polar_filter(raw, filters, out, r):
    channels = raw.shape[0] // filters.shape[0]
    out[r, :channels, :] = jnp.dot(
        raw[row_of(r, channels), :], filters[r], preferred_element_type=f32
    ).astype(bf16)


def gelu_parts(h, both=True):
    square = h * h
    half = 0.5 + 0.5 * jnp.tanh(h * (gelu_scale + (gelu_scale * gelu_cubic) * square))
    return half, h * (2.0 * gelu_scale + (6.0 * gelu_scale * gelu_cubic) * square) if both else None


def gelu_slope(half, lean):
    return half * (1.0 + (1.0 - half) * lean)


def control_kernel(*refs):
    first_halo, own, second_halo = refs[:3]
    refs = refs[3:]
    other = None
    if len(refs) > 19:
        other, refs = refs[:3], refs[3:]
    (
        taps, gain, bias, w_in, w_out, land, filters,
        out, unit_out, scale_out, slope_out, conv, normed, normed_b, hidden, hidden_b, act, act_b, raw,
    ) = refs
    rows, channels, width = out.shape
    hid = w_in.shape[0]
    normed, hidden, act = (normed, normed_b), (hidden, hidden_b), (act, act_b)
    odd = lax.axis_index("mem") % 2 == 1
    for block in normed:
        add_bias_rows(block, channels)
    blocks = [read(first_halo), read(own), read(second_halo)]
    if other is not None:
        blocks = [choose(odd, a, b) for a, b in zip((first_halo, own, second_halo), other)]
    convolve(*blocks, taps, conv, 10 if other is not None else 2)
    across = width // LANES

    def first(slot, r, at):
        for w in range(0, LANES, 128):
            here, there = slice(at.start + w, at.start + w + 128), slice(w, w + 128)
            value = conv[r, :, here]
            centered = value - jnp.mean(value, axis=0, keepdims=True)
            scale = lax.rsqrt(jnp.mean(centered * centered, axis=0, keepdims=True) + epsilon)
            unit = centered * scale
            unit_out[r, :, here] = unit
            scale_out[r, :, here] = scale
            normed[slot][:channels, there] = (unit * gain[...] + bias[...]).astype(bf16)
        hidden[slot][...] = jnp.dot(w_in[...], normed[slot][...], preferred_element_type=f32)

    def pair(slot, r, at):
        for c in range(0, hid, CHUNK):
            h = hidden[slot][c : c + CHUNK, :]
            half, lean = gelu_parts(h, other is None)
            act[slot][c : c + CHUNK, :] = (h * half).astype(bf16)
            if other is None:
                slope_out[r, c : c + CHUNK, at] = gelu_slope(half, lean)
            else:
                slope_out[r, c : c + CHUNK, at] = h

    def third(slot, r, at):
        update = jnp.dot(w_out[...], act[slot][...], preferred_element_type=f32)
        field = own[r, :, at]
        if other is not None:
            field = jnp.where(odd, other[1][r, :, at], field)
        raw[row_of(r, channels), at] = (land[pl.ds(r, 1), at] * (field.astype(f32) + update)).astype(bf16)
        if at.stop == width:
            polar_filter(raw, filters, out, r)

    pipeline(rows, across, other is None, first, pair, third)


def conv_kernel(first, own, second, taps, out):
    convolve(read(first), read(own), read(second), taps, out, 5)


def tangent_kernel(ready, *refs):
    if ready:
        own, conv = refs[:2]
        refs = refs[2:]
    else:
        near, own, far, taps = refs[:4]
        refs = refs[4:]
    gain, w_in, w_out, land, filters, unit_in, scale_in, slope_in, advanced, out = refs[:10]
    refs = refs[10:]
    if not ready:
        conv, refs = refs[0], refs[1:]
    normed, normed_b, hidden, hidden_b, act, act_b, raw = refs
    normed, hidden, act = (normed, normed_b), (hidden, hidden_b), (act, act_b)
    rows, channels, width = advanced.shape
    hid = w_in.shape[0]
    across = width // LANES
    is_control = lax.axis_index("mem") == 0

    def first(slot, r, at):
        for w in range(0, LANES, 128):
            here, there = slice(at.start + w, at.start + w + 128), slice(w, w + 128)
            value = conv[r, :, here]
            unit = unit_in[r, :, here]
            average = jnp.mean(value, axis=0, keepdims=True)
            along = jnp.mean(value * unit, axis=0, keepdims=True)
            normed[slot][:, there] = (gain[...] * scale_in[r, :, here] * (value - average - unit * along)).astype(bf16)
        hidden[slot][...] = jnp.dot(w_in[:, :channels], normed[slot][...], preferred_element_type=f32)

    def mix(slot, r, at):
        for c in range(0, hid, CHUNK):
            slope = slope_in[r, c : c + CHUNK, at]
            if ready:
                slope = gelu_slope(*gelu_parts(slope))
            act[slot][c : c + CHUNK, :] = (slope * hidden[slot][c : c + CHUNK, :]).astype(bf16)

    def third(slot, r, at):
        update = jnp.dot(w_out[...], act[slot][...], preferred_element_type=f32)
        raw[row_of(r, channels), at] = (
            land[pl.ds(r, 1), at] * (own[r, :channels, at].astype(f32) + update)
        ).astype(bf16)
        if at.stop == width:
            polar_filter(raw, filters, out, r)

    @pl.when(is_control)
    def _():
        out[:, :channels, :] = advanced[...]

    @pl.when(jnp.logical_not(is_control))
    def _():
        if not ready:
            convolve(read(near), read(own), read(far), taps, conv)
        pipeline(rows, across, False, first, mix, third)


def scratch(rows, channels, width, hid, bias_rows, conv=True):
    return ([pltpu.VMEM((rows, channels, width), f32)] if conv else []) + [
        pltpu.VMEM((channels + bias_rows, LANES), bf16),
        pltpu.VMEM((channels + bias_rows, LANES), bf16),
        pltpu.VMEM((hid, LANES), f32),
        pltpu.VMEM((hid, LANES), f32),
        pltpu.VMEM((hid, LANES), bf16),
        pltpu.VMEM((hid, LANES), bf16),
        pltpu.VMEM((rows * channels, width), bf16),
    ]


SMEM = pl.BlockSpec(memory_space=pltpu.SMEM)
VMEM = pl.BlockSpec(memory_space=pltpu.VMEM)
LIMIT = 24 << 20


def per_device(
    states, land_mask, cutoff, kernel, norm_gain, norm_bias, weight_in, bias_in, weight_out
):
    member = states[0]
    rows, channels, width = member.shape
    hid = weight_in.shape[1]
    bands = lax.axis_size("lat")
    members = lax.axis_size("mem")
    me = lax.axis_index("mem")
    params = pltpu.CompilerParams(vmem_limit_bytes=LIMIT)

    def shape(*dims, kind=f32):
        return jax.ShapeDtypeStruct(dims, kind)

    field = shape(rows, channels, width, kind=bf16)

    def send(block, pairs):
        return lax.ppermute(block, ("mem", "lat"), [(a * bands + i, b * bands + j) for (a, i), (b, j) in pairs])

    def neighbours(which, start):
        pairs = [((m, z), (m, z + 1)) for m in which for z in range(start, bands - 1, 2)]
        return pairs + [(b, a) for a, b in pairs]

    def exchange(block, which):
        even, odd = [m for m in which if m % 2 == 0], [m for m in which if m % 2 == 1]
        first = send(block, neighbours(even, 0) + neighbours(odd, 1))
        return first, send(block, neighbours(even, 1) + neighbours(odd, 0))

    def across(block, pairs):
        return send(block, [((a, z), (b, z)) for a, b in pairs for z in range(bands)])

    evens = list(range(0, members, 2))
    odds = list(range(1, members, 2))
    partners = [(m - 1, m) for m in odds]
    swapped = partners + [(b, a) for a, b in partners]

    table = jnp.asarray(fourier(width))
    w_out = weight_out.T
    sources = (kernel, norm_gain[None], norm_bias[None], weight_in, bias_in.reshape(-1, 128), land_mask)
    taps, gain, offset, w_in, land = pl.pallas_call(
        prepare_kernel,
        out_shape=(
            shape(rows, TAPS, channels, (rows + 2 * HALO) * GROUP, kind=bf16),
            shape(channels, 128),
            shape(channels, 128),
            shape(hid, channels + BIAS_ROWS, kind=bf16),
            shape(rows, width),
        ),
        in_specs=[pl.BlockSpec(memory_space=pltpu.MemorySpace.HBM)] * 6,
        out_specs=(VMEM,) * 5,
        scratch_shapes=[pltpu.VMEM(x.shape, x.dtype) for x in sources] + [pltpu.SemaphoreType.DMA((6,))],
        compiler_params=params,
        name="prepare",
    )(*sources)
    filters = pl.pallas_call(
        lambda *refs: filter_kernel(bands, *refs),
        out_shape=shape(rows, width, width, kind=bf16),
        in_specs=[SMEM, VMEM],
        out_specs=VMEM,
        compiler_params=params,
        name="filters",
    )(cutoff, table)

    def control_step(*halos):
        return pl.pallas_call(
            control_kernel,
            out_shape=(field, shape(rows, channels, width), shape(rows, 1, width), shape(rows, hid, width)),
            in_specs=[VMEM] * (7 + len(halos)),
            out_specs=(VMEM,) * 4,
            scratch_shapes=scratch(rows, channels, width, hid, BIAS_ROWS),
            compiler_params=params,
            name="control",
        )(*halos, taps, gain, offset, w_in, w_out, land, filters)

    def conv_step(near, own, far):
        return pl.pallas_call(
            conv_kernel,
            out_shape=shape(rows, channels, width),
            in_specs=[VMEM] * 4,
            out_specs=VMEM,
            compiler_params=params,
            name="conv",
        )(near, own, far, taps)

    def tangent_step(ready, inputs, unit, scale, slope, advanced):
        return pl.pallas_call(
            lambda *refs: tangent_kernel(ready, *refs),
            out_shape=field,
            in_specs=[VMEM] * (9 + len(inputs)),
            out_specs=VMEM,
            scratch_shapes=scratch(rows, channels, width, hid, 0, not ready),
            compiler_params=params,
            name="tangent",
        )(*inputs, gain, w_in, w_out, land, filters, unit, scale, slope, advanced)

    near, far = exchange(member, range(1, members))
    control = member
    count = 2
    while count < members:
        sent = across(control, [(m, m + count) for m in range(0, count, 2) if m + count < members])
        control = jnp.where((me >= count) & (me < 2 * count), sent, control)
        count *= 2
    control, taps = lax.optimization_barrier((control, taps))
    control_other = across(control, partners)
    control_near, control_far = exchange(control, evens)
    conv = conv_step(near, member, far)
    control_near, control_far, conv, filters = lax.optimization_barrier((control_near, control_far, conv, filters))
    other = (across(control_far, partners), control_other, across(control_near, partners))
    control, unit, scale, slope = control_step(control_near, control, control_far, *other)
    for step in range(1, STEPS):
        halo = exchange(control, range(members))[0]
        inputs = (member, conv) if step == 1 else (near, member, far, taps)
        member = tangent_step(step == 1, inputs, unit, scale, slope, control)
        halo, _ = lax.optimization_barrier((halo, member))
        halves = [across(part, swapped) for part in jnp.split(halo, 2, axis=1)]
        other = jnp.concatenate(halves, axis=1)
        near, far = exchange(member, range(1, members))
        control, unit, scale, slope = control_step(halo, control, other)
    return tangent_step(False, (near, member, far, taps), unit, scale, slope, control)[None]


def solution(mesh):
    in_specs = (
        P(("runs", "mem"), "lat", None, None),
        P("lat", None),
        P(),
        P(),
        P(),
        P(),
        P(),
        P(),
        P(),
    )
    out_specs = P(("runs", "mem"), "lat", None, None)
    return jax.shard_map(
        per_device, mesh=mesh, in_specs=in_specs, out_specs=out_specs, check_vma=False
    )
```

```python
import math

import jax
import jax.numpy as jnp
import numpy as np
from jax import lax
from jax.experimental import pallas as pl
from jax.experimental.pallas import tpu as pltpu
from jax.sharding import PartitionSpec as P

STEPS = 2
POLAR = 6
HALO = 3
TAPS = 7
GROUP = 16
LANES = 256
CHUNK = 64
BIAS_ROWS = 16

gelu_scale = 0.7978845608028654
gelu_cubic = 0.044715
epsilon = 1e-05

f32 = jnp.float32
bf16 = jnp.bfloat16


def fourier(width):
    index = np.arange(width, dtype=np.int32)
    wavenumber = np.where(index <= width // 2, index, index - width // 2).astype(np.int32)
    phase = index[:, None] * wavenumber[None, :] % width
    angle = phase.astype(np.float64) * (2.0 * math.pi / width)
    factor = np.where((index == 0) | (index == width // 2), 1.0 / math.sqrt(width), math.sqrt(2.0 / width))
    table = np.where(index[None, :] <= width // 2, np.cos(angle), np.sin(angle)) * factor[None, :]
    return table.astype(np.float32).astype(bf16)


def unroll(count, most):
    return max(u for u in range(1, most + 1) if count % u == 0)


def prepare_kernel(*refs):
    sources, refs = refs[:6], refs[6:]
    taps, gain_out, offset_out, w_in, land = refs[:5]
    kernel, gain, offset, weight_in, bias, land_mask, arrived = refs[5:]
    copies = [
        pltpu.make_async_copy(source, here, arrived.at[i])
        for i, (source, here) in enumerate(zip(sources, (kernel, gain, offset, weight_in, bias, land_mask)))
    ]
    for copy in copies:
        copy.start()
    for copy in copies:
        copy.wait()
    rows, _, channels, depth = taps.shape
    band = lax.axis_index("lat")
    lane = lax.broadcasted_iota(jnp.int32, (channels, depth), 1)
    here = lax.broadcasted_iota(jnp.int32, (channels, depth), 0)
    block = lane // GROUP
    turned = jnp.where(block < HALO, block + rows + HALO, jnp.where(block < HALO + rows, block, block - rows - HALO))
    block = jnp.where((band + lax.axis_index("mem")) % 2 == 1, block, turned)
    block = jnp.where(lane % GROUP == here % GROUP, block, -1)
    for j in range(TAPS):
        lines = [kernel[i, j : j + 1, :] for i in range(TAPS)] + [jnp.zeros((128 - TAPS, channels), f32)]
        turned = jnp.concatenate(lines, axis=0).T
        columns = [jnp.broadcast_to(turned[:, i : i + 1], (channels, depth)) for i in range(TAPS)]
        for r in range(rows):
            total = jnp.zeros((channels, depth), f32)
            for i in range(TAPS):
                total = jnp.where(block == r + i, columns[i], total)
            taps[r, j] = total.astype(bf16)
    gain_out[...] = jnp.broadcast_to(gain[...], (128, channels)).T
    offset_out[...] = jnp.broadcast_to(offset[...], (128, channels)).T
    w_in[:, :channels] = weight_in[...].astype(f32).T.astype(bf16)
    place = lax.broadcasted_iota(jnp.int32, (128, 128), 1)
    for k in range(bias.shape[0]):
        value = jnp.broadcast_to(bias[k : k + 1, :], (128, 128)).T
        high = value.astype(bf16).astype(f32)
        middle = (value - high).astype(bf16).astype(f32)
        low = value - high - middle
        three = jnp.where(place == 0, high, jnp.where(place == 1, middle, jnp.where(place == 2, low, 0.0)))
        w_in[k * 128 : (k + 1) * 128, channels:] = three[:, :BIAS_ROWS].astype(bf16)
    land[...] = land_mask[...].astype(f32)


def filter_kernel(bands, cutoff, table, out):
    rows, width, _ = out.shape
    band = lax.axis_index("lat")
    index = lax.broadcasted_iota(jnp.int32, (1, width), 1)
    wavenumber = jnp.where(index <= width // 2, index, index - width // 2)
    total_rows = rows * bands
    for r in range(rows):
        row = band * rows + r
        place = jnp.clip(jnp.where(row < POLAR, row, row - total_rows + 2 * POLAR), 0, 2 * POLAR - 1)
        kept = (table[...].astype(f32) * (wavenumber <= cutoff[place]).astype(f32)).astype(bf16)
        out[r] = lax.dot_general(
            kept, table[...], (((1,), (1,)), ((), ())), preferred_element_type=f32
        ).astype(bf16)
        if total_rows > 2 * POLAR:
            @pl.when((row >= POLAR) & (row < total_rows - POLAR))
            def _():
                across = lax.broadcasted_iota(jnp.int32, (width, width), 1)
                along = lax.broadcasted_iota(jnp.int32, (width, width), 0)
                out[r] = (across == along).astype(f32).astype(bf16)


def convolve(first, own, second, taps, out, most=10):
    rows, channels, width = out.shape

    def group(b, _):
        at = pl.ds(pl.multiple_of(b * GROUP, GROUP), GROUP)
        field = jnp.concatenate([first(at), own(at), second(at)], axis=0)
        field = field.reshape((rows + 2 * HALO) * GROUP, width)
        parts = jnp.dot(taps[:, :, at, :].reshape(rows * TAPS * GROUP, field.shape[0]), field, preferred_element_type=f32)
        for r in range(rows):
            part = [parts[(r * TAPS + j) * GROUP : (r * TAPS + j + 1) * GROUP] for j in range(TAPS)]
            total = part[HALO]
            for j in range(TAPS):
                if j != HALO:
                    total = total + pltpu.roll(part[j], (HALO - j) % width, 1)
            out[r, at, :] = total
        return 0

    groups = channels // GROUP
    lax.fori_loop(0, groups, group, 0, unroll=unroll(groups, most))


def read(ref):
    return lambda at: ref[:, at, :]


def choose(odd, first, other):
    return lambda at: jnp.where(odd, other[:, at, :], first[:, at, :])


def pipeline(rows, across, compact, first, second, third):
    def run(tiles):
        for i in range(len(tiles) + 2):
            for stage, lag in ((first, 0), (second, 1), (third, 2)):
                if lag <= i < len(tiles) + lag:
                    r, c = tiles[i - lag]
                    stage((i - lag) % 2, r, slice(c * LANES, (c + 1) * LANES))

    if compact:

        def one(r, _):
            run([(r, c) for c in range(across)])
            return 0

        lax.fori_loop(0, rows, one, 0)
    else:
        run([(r, c) for r in range(rows) for c in range(across)])


def row_of(r, channels):
    return pl.ds(pl.multiple_of(r * channels, GROUP), channels)


def add_bias_rows(normed, channels):
    row = lax.broadcasted_iota(jnp.int32, (BIAS_ROWS, normed.shape[1]), 0)
    normed[channels:, :] = jnp.where(row < 3, 1.0, 0.0).astype(bf16)


def polar_filter(raw, filters, out, r):
    channels = raw.shape[0] // filters.shape[0]
    out[r, :channels, :] = jnp.dot(
        raw[row_of(r, channels), :], filters[r], preferred_element_type=f32
    ).astype(bf16)


def gelu_parts(h, both=True):
    square = h * h
    half = 0.5 + 0.5 * jnp.tanh(h * (gelu_scale + (gelu_scale * gelu_cubic) * square))
    return half, h * (2.0 * gelu_scale + (6.0 * gelu_scale * gelu_cubic) * square) if both else None


def gelu_slope(half, lean):
    return half * (1.0 + (1.0 - half) * lean)


def control_kernel(*refs):
    first_halo, own, second_halo = refs[:3]
    refs = refs[3:]
    other = None
    if len(refs) > 19:
        other, refs = refs[:3], refs[3:]
    (
        taps, gain, bias, w_in, w_out, land, filters,
        out, unit_out, scale_out, slope_out, conv, normed, normed_b, hidden, hidden_b, act, act_b, raw,
    ) = refs
    rows, channels, width = out.shape
    hid = w_in.shape[0]
    normed, hidden, act = (normed, normed_b), (hidden, hidden_b), (act, act_b)
    odd = lax.axis_index("mem") % 2 == 1
    for block in normed:
        add_bias_rows(block, channels)
    blocks = [read(first_halo), read(own), read(second_halo)]
    if other is not None:
        blocks = [choose(odd, a, b) for a, b in zip((first_halo, own, second_halo), other)]
    convolve(*blocks, taps, conv, 10 if other is not None else 2)
    across = width // LANES

    def first(slot, r, at):
        for w in range(0, LANES, 128):
            here, there = slice(at.start + w, at.start + w + 128), slice(w, w + 128)
            value = conv[r, :, here]
            centered = value - jnp.mean(value, axis=0, keepdims=True)
            scale = lax.rsqrt(jnp.mean(centered * centered, axis=0, keepdims=True) + epsilon)
            unit = centered * scale
            unit_out[r, :, here] = unit
            scale_out[r, :, here] = scale
            normed[slot][:channels, there] = (unit * gain[...] + bias[...]).astype(bf16)
        hidden[slot][...] = jnp.dot(w_in[...], normed[slot][...], preferred_element_type=f32)

    def pair(slot, r, at):
        for c in range(0, hid, CHUNK):
            h = hidden[slot][c : c + CHUNK, :]
            half, lean = gelu_parts(h, other is None)
            act[slot][c : c + CHUNK, :] = (h * half).astype(bf16)
            if other is None:
                slope_out[r, c : c + CHUNK, at] = gelu_slope(half, lean)
            else:
                slope_out[r, c : c + CHUNK, at] = h

    def third(slot, r, at):
        update = jnp.dot(w_out[...], act[slot][...], preferred_element_type=f32)
        field = own[r, :, at]
        if other is not None:
            field = jnp.where(odd, other[1][r, :, at], field)
        raw[row_of(r, channels), at] = (land[pl.ds(r, 1), at] * (field.astype(f32) + update)).astype(bf16)
        if at.stop == width:
            polar_filter(raw, filters, out, r)

    pipeline(rows, across, other is None, first, pair, third)


def conv_kernel(first, own, second, taps, out):
    convolve(read(first), read(own), read(second), taps, out, 5)


def tangent_kernel(ready, *refs):
    if ready:
        own, conv = refs[:2]
        refs = refs[2:]
    else:
        near, own, far, taps = refs[:4]
        refs = refs[4:]
    gain, w_in, w_out, land, filters, unit_in, scale_in, slope_in, advanced, out = refs[:10]
    refs = refs[10:]
    if not ready:
        conv, refs = refs[0], refs[1:]
    normed, normed_b, hidden, hidden_b, act, act_b, raw = refs[:7]
    if not ready:
        done, sent = refs[7:]
    else:
        done = out
    normed, hidden, act = (normed, normed_b), (hidden, hidden_b), (act, act_b)
    rows, channels, width = advanced.shape
    hid = w_in.shape[0]
    across = width // LANES
    is_control = lax.axis_index("mem") == 0

    def first(slot, r, at):
        for w in range(0, LANES, 128):
            here, there = slice(at.start + w, at.start + w + 128), slice(w, w + 128)
            value = conv[r, :, here]
            unit = unit_in[r, :, here]
            average = jnp.mean(value, axis=0, keepdims=True)
            along = jnp.mean(value * unit, axis=0, keepdims=True)
            normed[slot][:, there] = (gain[...] * scale_in[r, :, here] * (value - average - unit * along)).astype(bf16)
        hidden[slot][...] = jnp.dot(w_in[:, :channels], normed[slot][...], preferred_element_type=f32)

    def mix(slot, r, at):
        for c in range(0, hid, CHUNK):
            slope = slope_in[r, c : c + CHUNK, at]
            if ready:
                slope = gelu_slope(*gelu_parts(slope))
            act[slot][c : c + CHUNK, :] = (slope * hidden[slot][c : c + CHUNK, :]).astype(bf16)

    def third(slot, r, at):
        update = jnp.dot(w_out[...], act[slot][...], preferred_element_type=f32)
        raw[row_of(r, channels), at] = (
            land[pl.ds(r, 1), at] * (own[r, :channels, at].astype(f32) + update)
        ).astype(bf16)
        if at.stop == width:
            polar_filter(raw, filters, done, r)
            if not ready:
                pltpu.make_async_copy(done.at[r], out.at[r], sent.at[r]).start()

    @pl.when(is_control)
    def _():
        done[...] = advanced[...]
        if not ready:
            for r in range(rows):
                pltpu.make_async_copy(done.at[r], out.at[r], sent.at[r]).start()

    @pl.when(jnp.logical_not(is_control))
    def _():
        if not ready:
            convolve(read(near), read(own), read(far), taps, conv)
        pipeline(rows, across, False, first, mix, third)

    if not ready:
        for r in range(rows):
            pltpu.make_async_copy(done.at[r], out.at[r], sent.at[r]).wait()


def scratch(rows, channels, width, hid, bias_rows, conv=True):
    return ([pltpu.VMEM((rows, channels, width), f32)] if conv else []) + [
        pltpu.VMEM((channels + bias_rows, LANES), bf16),
        pltpu.VMEM((channels + bias_rows, LANES), bf16),
        pltpu.VMEM((hid, LANES), f32),
        pltpu.VMEM((hid, LANES), f32),
        pltpu.VMEM((hid, LANES), bf16),
        pltpu.VMEM((hid, LANES), bf16),
        pltpu.VMEM((rows * channels, width), bf16),
    ]


SMEM = pl.BlockSpec(memory_space=pltpu.SMEM)
VMEM = pl.BlockSpec(memory_space=pltpu.VMEM)
LIMIT = 24 << 20


def per_device(
    states, land_mask, cutoff, kernel, norm_gain, norm_bias, weight_in, bias_in, weight_out
):
    member = states[0]
    rows, channels, width = member.shape
    hid = weight_in.shape[1]
    bands = lax.axis_size("lat")
    members = lax.axis_size("mem")
    me = lax.axis_index("mem")
    params = pltpu.CompilerParams(vmem_limit_bytes=LIMIT)

    def shape(*dims, kind=f32):
        return jax.ShapeDtypeStruct(dims, kind)

    field = shape(rows, channels, width, kind=bf16)

    def send(block, pairs):
        return lax.ppermute(block, ("mem", "lat"), [(a * bands + i, b * bands + j) for (a, i), (b, j) in pairs])

    def neighbours(which, start):
        pairs = [((m, z), (m, z + 1)) for m in which for z in range(start, bands - 1, 2)]
        return pairs + [(b, a) for a, b in pairs]

    def exchange(block, which):
        even, odd = [m for m in which if m % 2 == 0], [m for m in which if m % 2 == 1]
        first = send(block, neighbours(even, 0) + neighbours(odd, 1))
        return first, send(block, neighbours(even, 1) + neighbours(odd, 0))

    def across(block, pairs):
        return send(block, [((a, z), (b, z)) for a, b in pairs for z in range(bands)])

    evens = list(range(0, members, 2))
    odds = list(range(1, members, 2))
    partners = [(m - 1, m) for m in odds]
    swapped = partners + [(b, a) for a, b in partners]

    table = jnp.asarray(fourier(width))
    w_out = weight_out.T
    sources = (kernel, norm_gain[None], norm_bias[None], weight_in, bias_in.reshape(-1, 128), land_mask)
    taps, gain, offset, w_in, land = pl.pallas_call(
        prepare_kernel,
        out_shape=(
            shape(rows, TAPS, channels, (rows + 2 * HALO) * GROUP, kind=bf16),
            shape(channels, 128),
            shape(channels, 128),
            shape(hid, channels + BIAS_ROWS, kind=bf16),
            shape(rows, width),
        ),
        in_specs=[pl.BlockSpec(memory_space=pltpu.MemorySpace.HBM)] * 6,
        out_specs=(VMEM,) * 5,
        scratch_shapes=[pltpu.VMEM(x.shape, x.dtype) for x in sources] + [pltpu.SemaphoreType.DMA((6,))],
        compiler_params=params,
        name="prepare",
    )(*sources)
    filters = pl.pallas_call(
        lambda *refs: filter_kernel(bands, *refs),
        out_shape=shape(rows, width, width, kind=bf16),
        in_specs=[SMEM, VMEM],
        out_specs=VMEM,
        compiler_params=params,
        name="filters",
    )(cutoff, table)

    def control_step(*halos):
        return pl.pallas_call(
            control_kernel,
            out_shape=(field, shape(rows, channels, width), shape(rows, 1, width), shape(rows, hid, width)),
            in_specs=[VMEM] * (7 + len(halos)),
            out_specs=(VMEM,) * 4,
            scratch_shapes=scratch(rows, channels, width, hid, BIAS_ROWS),
            compiler_params=params,
            name="control",
        )(*halos, taps, gain, offset, w_in, w_out, land, filters)

    def conv_step(near, own, far):
        return pl.pallas_call(
            conv_kernel,
            out_shape=shape(rows, channels, width),
            in_specs=[VMEM] * 4,
            out_specs=VMEM,
            compiler_params=params,
            name="conv",
        )(near, own, far, taps)

    def tangent_step(ready, inputs, unit, scale, slope, advanced):
        return pl.pallas_call(
            lambda *refs: tangent_kernel(ready, *refs),
            out_shape=field,
            in_specs=[VMEM] * (9 + len(inputs)),
            out_specs=VMEM if ready else pl.BlockSpec(memory_space=pl.ANY),
            scratch_shapes=scratch(rows, channels, width, hid, 0, not ready)
            + ([] if ready else [pltpu.VMEM(field.shape, bf16), pltpu.SemaphoreType.DMA((rows,))]),
            compiler_params=params,
            name="tangent",
        )(*inputs, gain, w_in, w_out, land, filters, unit, scale, slope, advanced)

    near, far = exchange(member, range(1, members))
    control = member
    count = 2
    while count < members:
        sent = across(control, [(m, m + count) for m in range(0, count, 2) if m + count < members])
        control = jnp.where((me >= count) & (me < 2 * count), sent, control)
        count *= 2
    control, taps = lax.optimization_barrier((control, taps))
    control_other = across(control, partners)
    control_near, control_far = exchange(control, evens)
    conv = conv_step(near, member, far)
    control_near, control_far, conv, filters = lax.optimization_barrier((control_near, control_far, conv, filters))
    other = (across(control_far, partners), control_other, across(control_near, partners))
    control, unit, scale, slope = control_step(control_near, control, control_far, *other)
    for step in range(1, STEPS):
        halo = exchange(control, range(members))[0]
        inputs = (member, conv) if step == 1 else (near, member, far, taps)
        member = tangent_step(step == 1, inputs, unit, scale, slope, control)
        halo, _ = lax.optimization_barrier((halo, member))
        halves = [across(part, swapped) for part in jnp.split(halo, 2, axis=1)]
        other = jnp.concatenate(halves, axis=1)
        near, far = exchange(member, range(1, members))
        control, unit, scale, slope = control_step(halo, control, other)
    return tangent_step(False, (near, member, far, taps), unit, scale, slope, control)[None]


def solution(mesh):
    in_specs = (
        P(("runs", "mem"), "lat", None, None),
        P("lat", None),
        P(),
        P(),
        P(),
        P(),
        P(),
        P(),
        P(),
    )
    out_specs = P(("runs", "mem"), "lat", None, None)
    return jax.shard_map(
        per_device, mesh=mesh, in_specs=in_specs, out_specs=out_specs, check_vma=False
    )
```

```python
import math

import jax
import jax.numpy as jnp
import numpy as np
from jax import lax
from jax.experimental import pallas as pl
from jax.experimental.pallas import tpu as pltpu
from jax.sharding import PartitionSpec as P

STEPS = 2
POLAR = 6
HALO = 3
TAPS = 7
GROUP = 16
LANES = 256
CHUNK = 64
BIAS_ROWS = 16

gelu_scale = 0.7978845608028654
gelu_cubic = 0.044715
epsilon = 1e-05

f32 = jnp.float32
bf16 = jnp.bfloat16


def fourier(width):
    index = np.arange(width, dtype=np.int32)
    wavenumber = np.where(index <= width // 2, index, index - width // 2).astype(np.int32)
    phase = index[:, None] * wavenumber[None, :] % width
    angle = phase.astype(np.float64) * (2.0 * math.pi / width)
    factor = np.where((index == 0) | (index == width // 2), 1.0 / math.sqrt(width), math.sqrt(2.0 / width))
    table = np.where(index[None, :] <= width // 2, np.cos(angle), np.sin(angle)) * factor[None, :]
    return table.astype(np.float32).astype(bf16)


def unroll(count, most):
    return max(u for u in range(1, most + 1) if count % u == 0)


def prepare_kernel(*refs):
    sources, refs = refs[:6], refs[6:]
    taps, gain_out, offset_out, w_in, land = refs[:5]
    kernel, gain, offset, weight_in, bias, land_mask, arrived = refs[5:]
    copies = [
        pltpu.make_async_copy(source, here, arrived.at[i])
        for i, (source, here) in enumerate(zip(sources, (kernel, gain, offset, weight_in, bias, land_mask)))
    ]
    for copy in copies:
        copy.start()
    for copy in copies:
        copy.wait()
    rows, _, channels, depth = taps.shape
    band = lax.axis_index("lat")
    lane = lax.broadcasted_iota(jnp.int32, (channels, depth), 1)
    here = lax.broadcasted_iota(jnp.int32, (channels, depth), 0)
    block = lane // GROUP
    turned = jnp.where(block < HALO, block + rows + HALO, jnp.where(block < HALO + rows, block, block - rows - HALO))
    block = jnp.where((band + lax.axis_index("mem")) % 2 == 1, block, turned)
    block = jnp.where(lane % GROUP == here % GROUP, block, -1)
    for j in range(TAPS):
        lines = [kernel[i, j : j + 1, :] for i in range(TAPS)] + [jnp.zeros((128 - TAPS, channels), f32)]
        turned = jnp.concatenate(lines, axis=0).T
        columns = [jnp.broadcast_to(turned[:, i : i + 1], (channels, depth)) for i in range(TAPS)]
        for r in range(rows):
            total = jnp.zeros((channels, depth), f32)
            for i in range(TAPS):
                total = jnp.where(block == r + i, columns[i], total)
            taps[r, j] = total.astype(bf16)
    gain_out[...] = jnp.broadcast_to(gain[...], (128, channels)).T
    offset_out[...] = jnp.broadcast_to(offset[...], (128, channels)).T
    w_in[:, :channels] = weight_in[...].astype(f32).T.astype(bf16)
    place = lax.broadcasted_iota(jnp.int32, (128, 128), 1)
    for k in range(bias.shape[0]):
        value = jnp.broadcast_to(bias[k : k + 1, :], (128, 128)).T
        high = value.astype(bf16).astype(f32)
        middle = (value - high).astype(bf16).astype(f32)
        low = value - high - middle
        three = jnp.where(place == 0, high, jnp.where(place == 1, middle, jnp.where(place == 2, low, 0.0)))
        w_in[k * 128 : (k + 1) * 128, channels:] = three[:, :BIAS_ROWS].astype(bf16)
    land[...] = land_mask[...].astype(f32)


def filter_kernel(bands, cutoff, table, out):
    rows, width, _ = out.shape
    band = lax.axis_index("lat")
    index = lax.broadcasted_iota(jnp.int32, (1, width), 1)
    wavenumber = jnp.where(index <= width // 2, index, index - width // 2)
    total_rows = rows * bands
    for r in range(rows):
        row = band * rows + r
        place = jnp.clip(jnp.where(row < POLAR, row, row - total_rows + 2 * POLAR), 0, 2 * POLAR - 1)
        kept = (table[...].astype(f32) * (wavenumber <= cutoff[place]).astype(f32)).astype(bf16)
        out[r] = lax.dot_general(
            kept, table[...], (((1,), (1,)), ((), ())), preferred_element_type=f32
        ).astype(bf16)
        if total_rows > 2 * POLAR:
            @pl.when((row >= POLAR) & (row < total_rows - POLAR))
            def _():
                across = lax.broadcasted_iota(jnp.int32, (width, width), 1)
                along = lax.broadcasted_iota(jnp.int32, (width, width), 0)
                out[r] = (across == along).astype(f32).astype(bf16)


def convolve(first, own, second, taps, out, most=10):
    rows, channels, width = out.shape

    def group(b, _):
        at = pl.ds(pl.multiple_of(b * GROUP, GROUP), GROUP)
        field = jnp.concatenate([first(at), own(at), second(at)], axis=0)
        field = field.reshape((rows + 2 * HALO) * GROUP, width)
        parts = jnp.dot(taps[:, :, at, :].reshape(rows * TAPS * GROUP, field.shape[0]), field, preferred_element_type=f32)
        for r in range(rows):
            part = [parts[(r * TAPS + j) * GROUP : (r * TAPS + j + 1) * GROUP] for j in range(TAPS)]
            total = part[HALO]
            for j in range(TAPS):
                if j != HALO:
                    total = total + pltpu.roll(part[j], (HALO - j) % width, 1)
            out[r, at, :] = total
        return 0

    groups = channels // GROUP
    lax.fori_loop(0, groups, group, 0, unroll=unroll(groups, most))


def read(ref):
    return lambda at: ref[:, at, :]


def choose(odd, first, other):
    return lambda at: jnp.where(odd, other[:, at, :], first[:, at, :])


def pipeline(rows, across, compact, first, second, third):
    def run(tiles):
        for i in range(len(tiles) + 2):
            for stage, lag in ((first, 0), (second, 1), (third, 2)):
                if lag <= i < len(tiles) + lag:
                    r, c = tiles[i - lag]
                    stage((i - lag) % 2, r, slice(c * LANES, (c + 1) * LANES))

    if compact:

        def one(r, _):
            run([(r, c) for c in range(across)])
            return 0

        lax.fori_loop(0, rows, one, 0)
    else:
        run([(r, c) for r in range(rows) for c in range(across)])


def row_of(r, channels):
    return pl.ds(pl.multiple_of(r * channels, GROUP), channels)


def add_bias_rows(normed, channels):
    row = lax.broadcasted_iota(jnp.int32, (BIAS_ROWS, normed.shape[1]), 0)
    normed[channels:, :] = jnp.where(row < 3, 1.0, 0.0).astype(bf16)


def polar_filter(raw, filters, out, r):
    channels = raw.shape[0] // filters.shape[0]
    out[r, :channels, :] = jnp.dot(
        raw[row_of(r, channels), :], filters[r], preferred_element_type=f32
    ).astype(bf16)


def gelu_parts(h, both=True):
    square = h * h
    half = 0.5 + 0.5 * jnp.tanh(h * (gelu_scale + (gelu_scale * gelu_cubic) * square))
    return half, h * (2.0 * gelu_scale + (6.0 * gelu_scale * gelu_cubic) * square) if both else None


def gelu_slope(half, lean):
    return half * (1.0 + (1.0 - half) * lean)


def control_kernel(*refs):
    first_halo, own, second_halo = refs[:3]
    refs = refs[3:]
    other = None
    if len(refs) > 19:
        other, refs = refs[:3], refs[3:]
    (
        taps, gain, bias, w_in, w_out, land, filters,
        out, unit_out, scale_out, slope_out, conv, normed, normed_b, hidden, hidden_b, act, act_b, raw,
    ) = refs
    rows, channels, width = out.shape
    hid = w_in.shape[0]
    normed, hidden, act = (normed, normed_b), (hidden, hidden_b), (act, act_b)
    odd = lax.axis_index("mem") % 2 == 1
    for block in normed:
        add_bias_rows(block, channels)
    blocks = [read(first_halo), read(own), read(second_halo)]
    if other is not None:
        blocks = [choose(odd, a, b) for a, b in zip((first_halo, own, second_halo), other)]
    convolve(*blocks, taps, conv, 10 if other is not None else 2)
    across = width // LANES

    def first(slot, r, at):
        for w in range(0, LANES, 128):
            here, there = slice(at.start + w, at.start + w + 128), slice(w, w + 128)
            value = conv[r, :, here]
            centered = value - jnp.mean(value, axis=0, keepdims=True)
            scale = lax.rsqrt(jnp.mean(centered * centered, axis=0, keepdims=True) + epsilon)
            unit = centered * scale
            unit_out[r, :, here] = unit
            scale_out[r, :, here] = scale
            normed[slot][:channels, there] = (unit * gain[...] + bias[...]).astype(bf16)
        hidden[slot][...] = jnp.dot(w_in[...], normed[slot][...], preferred_element_type=f32)

    def pair(slot, r, at):
        for c in range(0, hid, CHUNK):
            h = hidden[slot][c : c + CHUNK, :]
            half, lean = gelu_parts(h, other is None)
            act[slot][c : c + CHUNK, :] = (h * half).astype(bf16)
            if other is None:
                slope_out[r, c : c + CHUNK, at] = gelu_slope(half, lean)
            else:
                slope_out[r, c : c + CHUNK, at] = h

    def third(slot, r, at):
        update = jnp.dot(w_out[...], act[slot][...], preferred_element_type=f32)
        field = own[r, :, at]
        if other is not None:
            field = jnp.where(odd, other[1][r, :, at], field)
        raw[row_of(r, channels), at] = (land[pl.ds(r, 1), at] * (field.astype(f32) + update)).astype(bf16)
        if at.stop == width:
            polar_filter(raw, filters, out, r)

    pipeline(rows, across, other is None, first, pair, third)


def conv_kernel(first, own, second, taps, out):
    convolve(read(first), read(own), read(second), taps, out, 5)


def tangent_kernel(ready, *refs):
    if ready:
        own, conv = refs[:2]
        refs = refs[2:]
    else:
        near, own, far, taps = refs[:4]
        refs = refs[4:]
    gain, w_in, w_out, land, filters, unit_in, scale_in, slope_in, advanced, out = refs[:10]
    refs = refs[10:]
    if not ready:
        conv, refs = refs[0], refs[1:]
    normed, normed_b, hidden, hidden_b, act, act_b, raw = refs
    normed, hidden, act = (normed, normed_b), (hidden, hidden_b), (act, act_b)
    rows, channels, width = advanced.shape
    hid = w_in.shape[0]
    across = width // LANES
    is_control = lax.axis_index("mem") == 0

    def first(slot, r, at):
        for w in range(0, LANES, 128):
            here, there = slice(at.start + w, at.start + w + 128), slice(w, w + 128)
            value = conv[r, :, here]
            unit = unit_in[r, :, here]
            average = jnp.mean(value, axis=0, keepdims=True)
            along = jnp.mean(value * unit, axis=0, keepdims=True)
            normed[slot][:, there] = (gain[...] * scale_in[r, :, here] * (value - average - unit * along)).astype(bf16)
        hidden[slot][...] = jnp.dot(w_in[:, :channels], normed[slot][...], preferred_element_type=f32)

    def mix(slot, r, at):
        for c in range(0, hid, CHUNK):
            slope = slope_in[r, c : c + CHUNK, at]
            if ready:
                slope = gelu_slope(*gelu_parts(slope))
            act[slot][c : c + CHUNK, :] = (slope * hidden[slot][c : c + CHUNK, :]).astype(bf16)

    def third(slot, r, at):
        update = jnp.dot(w_out[...], act[slot][...], preferred_element_type=f32)
        raw[row_of(r, channels), at] = (
            land[pl.ds(r, 1), at] * (own[r, :channels, at].astype(f32) + update)
        ).astype(bf16)
        if at.stop == width:
            polar_filter(raw, filters, out, r)

    @pl.when(is_control)
    def _():
        out[:, :channels, :] = advanced[...]

    @pl.when(jnp.logical_not(is_control))
    def _():
        if not ready:
            convolve(read(near), read(own), read(far), taps, conv)
        pipeline(rows, across, False, first, mix, third)


def scratch(rows, channels, width, hid, bias_rows, conv=True):
    return ([pltpu.VMEM((rows, channels, width), f32)] if conv else []) + [
        pltpu.VMEM((channels + bias_rows, LANES), bf16),
        pltpu.VMEM((channels + bias_rows, LANES), bf16),
        pltpu.VMEM((hid, LANES), f32),
        pltpu.VMEM((hid, LANES), f32),
        pltpu.VMEM((hid, LANES), bf16),
        pltpu.VMEM((hid, LANES), bf16),
        pltpu.VMEM((rows * channels, width), bf16),
    ]


SMEM = pl.BlockSpec(memory_space=pltpu.SMEM)
VMEM = pl.BlockSpec(memory_space=pltpu.VMEM)
LIMIT = 24 << 20


def per_device(
    states, land_mask, cutoff, kernel, norm_gain, norm_bias, weight_in, bias_in, weight_out
):
    member = states[0]
    rows, channels, width = member.shape
    hid = weight_in.shape[1]
    bands = lax.axis_size("lat")
    members = lax.axis_size("mem")
    me = lax.axis_index("mem")
    params = pltpu.CompilerParams(vmem_limit_bytes=LIMIT)

    def shape(*dims, kind=f32):
        return jax.ShapeDtypeStruct(dims, kind)

    field = shape(rows, channels, width, kind=bf16)

    def send(block, pairs):
        return lax.ppermute(block, ("mem", "lat"), [(a * bands + i, b * bands + j) for (a, i), (b, j) in pairs])

    def neighbours(which, start):
        pairs = [((m, z), (m, z + 1)) for m in which for z in range(start, bands - 1, 2)]
        return pairs + [(b, a) for a, b in pairs]

    def exchange(block, which):
        even, odd = [m for m in which if m % 2 == 0], [m for m in which if m % 2 == 1]
        first = send(block, neighbours(even, 0) + neighbours(odd, 1))
        return first, send(block, neighbours(even, 1) + neighbours(odd, 0))

    def across(block, pairs):
        return send(block, [((a, z), (b, z)) for a, b in pairs for z in range(bands)])

    def in_halves(block, pairs):
        return jnp.concatenate([across(part, pairs) for part in jnp.split(block, 2, axis=1)], axis=1)

    evens = list(range(0, members, 2))
    odds = list(range(1, members, 2))
    partners = [(m - 1, m) for m in odds]
    swapped = partners + [(b, a) for a, b in partners]

    table = jnp.asarray(fourier(width))
    w_out = weight_out.T
    sources = (kernel, norm_gain[None], norm_bias[None], weight_in, bias_in.reshape(-1, 128), land_mask)
    taps, gain, offset, w_in, land = pl.pallas_call(
        prepare_kernel,
        out_shape=(
            shape(rows, TAPS, channels, (rows + 2 * HALO) * GROUP, kind=bf16),
            shape(channels, 128),
            shape(channels, 128),
            shape(hid, channels + BIAS_ROWS, kind=bf16),
            shape(rows, width),
        ),
        in_specs=[pl.BlockSpec(memory_space=pltpu.MemorySpace.HBM)] * 6,
        out_specs=(VMEM,) * 5,
        scratch_shapes=[pltpu.VMEM(x.shape, x.dtype) for x in sources] + [pltpu.SemaphoreType.DMA((6,))],
        compiler_params=params,
        name="prepare",
    )(*sources)
    filters = pl.pallas_call(
        lambda *refs: filter_kernel(bands, *refs),
        out_shape=shape(rows, width, width, kind=bf16),
        in_specs=[SMEM, VMEM],
        out_specs=VMEM,
        compiler_params=params,
        name="filters",
    )(cutoff, table)

    def control_step(*halos):
        return pl.pallas_call(
            control_kernel,
            out_shape=(field, shape(rows, channels, width), shape(rows, 1, width), shape(rows, hid, width)),
            in_specs=[VMEM] * (7 + len(halos)),
            out_specs=(VMEM,) * 4,
            scratch_shapes=scratch(rows, channels, width, hid, BIAS_ROWS),
            compiler_params=params,
            name="control",
        )(*halos, taps, gain, offset, w_in, w_out, land, filters)

    def conv_step(near, own, far):
        return pl.pallas_call(
            conv_kernel,
            out_shape=shape(rows, channels, width),
            in_specs=[VMEM] * 4,
            out_specs=VMEM,
            compiler_params=params,
            name="conv",
        )(near, own, far, taps)

    def tangent_step(ready, inputs, unit, scale, slope, advanced):
        return pl.pallas_call(
            lambda *refs: tangent_kernel(ready, *refs),
            out_shape=field,
            in_specs=[VMEM] * (9 + len(inputs)),
            out_specs=VMEM,
            scratch_shapes=scratch(rows, channels, width, hid, 0, not ready),
            compiler_params=params,
            name="tangent",
        )(*inputs, gain, w_in, w_out, land, filters, unit, scale, slope, advanced)

    near, far = exchange(member, range(1, members))
    control = member
    count = 2
    while count < members:
        sent = across(control, [(m, m + count) for m in range(0, count, 2) if m + count < members])
        control = jnp.where((me >= count) & (me < 2 * count), sent, control)
        count *= 2
    control, taps = lax.optimization_barrier((control, taps))
    control_other = across(control, partners)
    control_near, control_far = exchange(control, evens)
    conv = conv_step(near, member, far)
    control_near, control_far, conv, filters = lax.optimization_barrier((control_near, control_far, conv, filters))
    other = (in_halves(control_far, partners), control_other, in_halves(control_near, partners))
    control, unit, scale, slope = control_step(control_near, control, control_far, *other)
    for step in range(1, STEPS):
        halo = exchange(control, range(members))[0]
        inputs = (member, conv) if step == 1 else (near, member, far, taps)
        member = tangent_step(step == 1, inputs, unit, scale, slope, control)
        halo, _ = lax.optimization_barrier((halo, member))
        other = in_halves(halo, swapped)
        near, far = exchange(member, range(1, members))
        control, unit, scale, slope = control_step(halo, control, other)
    return tangent_step(False, (near, member, far, taps), unit, scale, slope, control)[None]


def solution(mesh):
    in_specs = (
        P(("runs", "mem"), "lat", None, None),
        P("lat", None),
        P(),
        P(),
        P(),
        P(),
        P(),
        P(),
        P(),
    )
    out_specs = P(("runs", "mem"), "lat", None, None)
    return jax.shard_map(
        per_device, mesh=mesh, in_specs=in_specs, out_specs=out_specs, check_vma=False
    )
```
